128 devices in a mesh: lat: 4 (over x_lo, core), lon: 32 (over x_hi, y, z).
Axes of the slice: x: 4 (x_hi: 2, x_lo: 2; x = x_hi * 2 + x_lo), y: 4, z: 4, core: 2. Of those that a mesh axis runs over, the one named last changes fastest.
Arguments:
- air_temp: float32 [128, 2880, 128], P('lat', 'lon'), may hold values from -6 to 6
- sea_temp: float32 [128, 2880], P(('lat', 'lon')), may hold values from -6 to 6
- land_sea: int32 [128, 2880], P('lat', 'lon'), may hold values 0 or 1
- courant: float32 [128], replicated, may hold values from -0.4 to 0.4
- vertical_mix: float32 [128, 128], replicated, may hold values from -0.25 to 0.25
- cutoffs: int32 [32], replicated, may hold values from 1 to 127, as said below
Outputs:
- air_final: float32 [128, 2880, 128], P('lat', 'lon')
- sea_final: float32 [128, 2880], P(('lat', 'lon'))
The draws below stay inside these ranges and needn't reach their ends.
Inputs may be any that keep to these rules, and one draw needn't show every extreme that they name: cutoffs holds the rows in the order of the filtered rows; some row keeps exactly 127.
All inputs are finite; a program needn't handle non-finite values. No bound on the sum of `land_sea` on one device may be relied on, other than what follows from the above.
Results may differ from the reference program's by a relative error of at most 0.0001.
Values sent between devices are 32-bit elements; how exact they have to be, the bound alone decides.
A program may use at most 128 MiB of HBM per device.

```python
import math
import jax
import jax.numpy as jnp
from jax import lax

NLON = 2880
LEVELS = 128
NPOLE = 16
KMAX = 127
STEPS = 6
NLAT = 128


def draw_cutoffs(key, part):
    values = jax.random.randint(jax.random.fold_in(key, 7), (2 * NPOLE,), 1, KMAX + 1)
    return values.at[NPOLE - 1].set(KMAX).astype(jnp.int32)


def plant(result, stream_key, low, high):
    index_at = [jax.random.randint(jax.random.fold_in(stream_key, axis), (), 0, length) for axis, length in enumerate(result.shape)]
    main_axis = result.shape.index(max(result.shape))
    next_to = index_at[:main_axis] + [(index_at[main_axis] + 1) % result.shape[main_axis]] + index_at[main_axis + 1:]
    return result.at[tuple(index_at)].set(low).at[tuple(next_to)].set(high)


def steps_of(own_key, extent, shards, smallest, top_value):
    gain = 1.0
    for position, shards_of in shards:
        draws = jax.random.uniform(jax.random.fold_in(jax.random.fold_in(own_key, 6), position), (shards_of,), jnp.float32, smallest / len(shards), top_value / len(shards))
        gain = gain * jnp.repeat(jnp.exp(draws), extent[position] // shards_of).reshape((-1,) + (1,) * (len(extent) - 1 - position))
    return gain


def noise(own_key, extent, width, most, shards=(), kind=jnp.bfloat16):
    gain = steps_of(own_key, extent, shards, -0.22, 0.18) if shards else 1.0
    result = jax.random.normal(own_key, extent, jnp.float32) * width * gain
    return jnp.minimum(jnp.maximum(result, -most), most).astype(kind)


def setup_inputs(seed: int = 0) -> dict:
    arg_keys = jax.random.split(jax.random.key(seed), 7)
    return {
        "air_temp": noise(arg_keys[0], (NLAT, NLON, LEVELS), 1.0, 6.0, ((0, 4), (1, 32)), jnp.float32),
        "sea_temp": noise(arg_keys[1], (NLAT, NLON), 1.0, 6.0, ((0, 128),), jnp.float32),
        "land_sea": plant((jax.random.randint(arg_keys[2], (NLAT, NLON), 0, 3) < 2).astype(jnp.int32), jax.random.fold_in(arg_keys[2], 1), 0, 1),
        "courant": jnp.clip(jax.random.uniform(arg_keys[3], (LEVELS,), jnp.float32, -0.4, 0.4), -0.4, 0.4),
        "vertical_mix": noise(arg_keys[4], (LEVELS, LEVELS), (4 * LEVELS) ** -0.5, 0.25, (), jnp.float32),
        "cutoffs": draw_cutoffs(jax.random.fold_in(arg_keys[6], 71), 0),
    }


diffusion_rate = 0.1
air_gain = 0.5
ocean_gain = 0.3
ocean_diffusion = 0.2
sea_coef = 0.5
land_coef = 0.15


def horizontal(air_temp, courant):
    zero_row = jnp.zeros_like(air_temp[:1])
    north_cell = jnp.concatenate([zero_row, air_temp[:-1]], 0)
    south_cell = jnp.concatenate([air_temp[1:], zero_row], 0)
    east_cell = jnp.roll(air_temp, -1, axis=1)
    west_cell = jnp.roll(air_temp, 1, axis=1)
    laplace = north_cell + south_cell + east_cell + west_cell - 4.0 * air_temp
    return air_temp + diffusion_rate * laplace - 0.5 * courant * (east_cell - west_cell)


def polar_filter(polar_rows, cutoff):
    wavenum = jnp.arange(KMAX + 1, dtype=jnp.int32)
    columns = jnp.arange(NLON, dtype=jnp.int32)
    phase = ((columns[:, None] * wavenum[None, :]) % NLON).astype(jnp.float32) * (2.0 * math.pi / NLON)
    cosine = jnp.cos(phase)
    sine_table = jnp.sin(phase)
    real_part = jnp.einsum('pcl,ck->pkl', polar_rows, cosine, precision=lax.Precision.HIGHEST)
    imag_part = jnp.einsum('pcl,ck->pkl', polar_rows, sine_table, precision=lax.Precision.HIGHEST)
    weights = jnp.where(wavenum[None, :] <= cutoff[:, None], jnp.where(wavenum[None, :] == 0, 1.0, 2.0), 0.0) / NLON
    weights = weights[:, :, None]
    return (jnp.einsum('pkl,ck->pcl', real_part * weights, cosine, precision=lax.Precision.HIGHEST)
            + jnp.einsum('pkl,ck->pcl', imag_part * weights, sine_table, precision=lax.Precision.HIGHEST))


def reference(air_temp, sea_temp, land_sea, courant, vertical_mix, cutoffs):
    exchange_coef = jnp.where(land_sea == 1, sea_coef, land_coef)
    for step_index in range(STEPS):
        advanced = horizontal(air_temp, courant)
        polar_rows = jnp.concatenate([advanced[:NPOLE], advanced[NLAT - NPOLE:]], 0)
        filtered = polar_filter(polar_rows, cutoffs)
        advanced = advanced.at[:NPOLE].set(filtered[:NPOLE]).at[NLAT - NPOLE:].set(filtered[NPOLE:])
        mixed = jnp.dot(advanced.reshape(-1, LEVELS), vertical_mix, precision=lax.Precision.HIGHEST)
        air_next = advanced + mixed.reshape(advanced.shape)
        heat_flux = exchange_coef * (sea_temp - air_next[:, :, 0])
        air_temp = air_next.at[:, :, 0].add(air_gain * heat_flux)
        zero_row = jnp.zeros_like(sea_temp[:1])
        laplace = (jnp.concatenate([zero_row, sea_temp[:-1]], 0) + jnp.concatenate([sea_temp[1:], zero_row], 0)
                   + jnp.roll(sea_temp, 1, axis=1) + jnp.roll(sea_temp, -1, axis=1) - 4.0 * sea_temp)
        sea_temp = sea_temp - ocean_gain * heat_flux + ocean_diffusion * laplace
    return air_temp, sea_temp
```

```python
import functools

import jax
import jax.numpy as jnp
import ml_dtypes
import numpy as np
from jax import lax
from jax.experimental import pallas as pl
from jax.experimental.pallas import tpu as pltpu
from jax.sharding import PartitionSpec as P

STEPS = 6
NPOLE = 16
ROWS = 32
COLS = 90
KW = 128
LEV = 128
HALO = 6
FRAMES = 49
WIDE = 120
Q0, QN = 8, 104
SPEC = NPOLE + HALO
PACK = 24

f32, bf16 = jnp.float32, jnp.bfloat16
MESH = pl.DeviceIdType.MESH


def split(x):
    hi = x.astype(bf16)
    return hi, (x - hi.astype(f32)).astype(bf16)


def dot(a, b):
    return jnp.dot(a, b, preferred_element_type=f32)


def dot3(a, b):
    return dot(a[0], b[0]) + dot(a[1], b[0]) + dot(a[0], b[1])


def np_split(x):
    x = x.astype(np.float32)
    hi = x.astype(ml_dtypes.bfloat16)
    lo = (x - hi.astype(np.float32)).astype(ml_dtypes.bfloat16)
    return np.stack([hi, lo])


def tables(nl):
    nlon = nl * COLS
    k = np.arange(KW)

    def fwd(c):
        ang = (c[..., None] * k % nlon) * (2.0 * np.pi / nlon)
        return np.concatenate([np.cos(ang), np.sin(ang)], -1)

    weight = np.where(k == 0, 1.0, 2.0) / nlon
    weight = np.concatenate([weight, weight])
    d = np.arange(nl)[:, None]
    c = np.arange(96)[None]
    full = np.where((c < COLS)[..., None], fwd(d * COLS + c), 0.0)
    own = np.moveaxis(np_split(full.transpose(0, 2, 1)), 0, 1)
    q = np.arange(QN)[None]
    inv = np.moveaxis(np_split(fwd((d * COLS + q - 8) % nlon) * weight), 0, 1)
    packed = full.reshape(nl, 4, PACK, 256).transpose(1, 3, 0, 2).reshape(4, 256, nl * PACK)
    step = 2.0 * np.pi / nlon
    wave = np.stack([0.6 + 0.2 * np.cos(k * step), np.sin(k * step)])
    wave = np.broadcast_to(wave[:, :, None], (2, KW, LEV)).astype(np.float32)
    return own, inv, np_split(packed), wave


def kernel(nl, a_ref, seaw_ref, coef_ref, cour_ref, vmix_ref, cut_ref, own_hbm, inv_hbm, ct_hbm,
           wave_ref, out_ref, seaout_ref, fa, fb, sa, sb, part, rsb, fx, fp, halo, coefr, sear,
           seab, seaf, seafin, sendx, recvx, own, inv, ct, vb, mt, a0t, coeft, st0, st1, fluxt,
           s0t, wv, tsem, asem, csem, seas, searow, xsem, rssem, agsem, fxs, fins):
    lat, lon = lax.axis_index("lat"), lax.axis_index("lon")
    polar = jnp.logical_or(lat == 0, lat == 3)
    flip = lat == 3
    ko = 2 * KW // nl
    rp = ROWS // nl
    lane = lax.broadcasted_iota(jnp.int32, (QN, LEV), 1)

    def natural(m):
        return jnp.where(flip, ROWS - 1 - m, m)

    def peers(body):
        def one(i, carry):
            body(lax.rem(lon + i, nl))
            return carry
        lax.fori_loop(1, nl, one, 0)

    def wait_bytes(ref, sem):
        pltpu.make_async_copy(ref, ref, sem).wait()

    def to_lon(src, dst, ssem, rsem, peer):
        return pltpu.make_async_remote_copy(src, dst, ssem, rsem, device_id={"lon": peer},
                                            device_id_type=MESH)

    loads = [
        pltpu.make_async_copy(own_hbm.at[lon], own, tsem.at[0]),
        pltpu.make_async_copy(inv_hbm.at[lon], inv, tsem.at[1]),
        pltpu.make_async_copy(ct_hbm, ct, tsem.at[2]),
    ]

    @pl.when(polar)
    def _():
        for load in loads:
            load.start()

    barrier = pltpu.get_barrier_semaphore()
    peers(lambda p: pl.semaphore_signal(barrier, inc=1, device_id={"lon": p}, device_id_type=MESH))

    @pl.when(lat < 3)
    def _():
        pl.semaphore_signal(barrier, inc=1, device_id={"lat": lat + 1}, device_id_type=MESH)

    @pl.when(lat > 0)
    def _():
        pl.semaphore_signal(barrier, inc=1, device_id={"lat": lat - 1}, device_id_type=MESH)

    pl.semaphore_wait(barrier, nl - 1 + jnp.where(polar, 1, 2))

    side = jnp.where(lat == 2, 1, 0)

    def lat_sends(src_ref, dst_ref, sems):
        def make(src, s, i, which, to):
            return pltpu.make_async_remote_copy(
                src_ref.at[src], dst_ref.at[s, i], sems.at[which], sems.at[2 + s],
                device_id={"lat": to}, device_id_type=MESH)

        @pl.when(lat < 3)
        def _():
            for i in range(HALO):
                make(jnp.where(lat == 2, ROWS - 1 - i, ROWS - HALO + i), side, i, 0, lat + 1).start()

        @pl.when(lat > 0)
        def _():
            for i in range(HALO):
                make(i, 1, i, 1, lat - 1).start()

    def lat_recvs(dst_ref, sems):
        wait_bytes(dst_ref.at[1], sems.at[3])

        @pl.when(jnp.logical_not(polar))
        def _():
            wait_bytes(dst_ref.at[0], sems.at[2])

    def lat_sent(dst_ref, sems):
        @pl.when(lat < 3)
        def _():
            wait_bytes(dst_ref.at[0], sems.at[0])

        @pl.when(lat > 0)
        def _():
            wait_bytes(dst_ref.at[0], sems.at[1])

    peers(lambda p: to_lon(seaw_ref.at[p], seab.at[pl.ds(rp * lon, rp)], seas.at[0], seas.at[1], p).start())
    lat_sends(coef_ref, coefr, csem)
    lat_sends(a_ref, halo, asem)

    def own_sea(i, carry):
        seab[rp * lon + i] = seaw_ref[lon, i]
        return carry
    lax.fori_loop(0, rp, own_sea, 0)

    def clear(f, carry):
        z = jnp.zeros((8, LEV), f32)
        fa[f, pl.ds(0, 8), :] = z
        fa[f, pl.ds(WIDE - 16, 8), :] = z
        fa[f, pl.ds(WIDE - 8, 8), :] = z
        fb[f, pl.ds(0, 8), :] = z
        fb[f, pl.ds(WIDE - 8, 8), :] = z
        return carry
    lax.fori_loop(0, FRAMES, clear, 0)
    for f in (0, 1, 46, 47):
        fa[f] = jnp.zeros((WIDE, LEV), f32)
        fb[f] = jnp.zeros((WIDE, LEV), f32)
    fa[48] = jnp.zeros((WIDE, LEV), f32)
    fb[48] = jnp.zeros((WIDE, LEV), f32)

    def fill(m, carry):
        fa[m + 8, pl.ds(16, COLS), :] = a_ref[natural(m)]
        return carry
    lax.fori_loop(0, ROWS, fill, 0)

    @pl.when(polar)
    def _():
        loads[0].wait()
        tab = (own[0], own[1])

        def transform(i, carry):
            f = 8 + 2 * i
            rows = jnp.concatenate([fa[f, pl.ds(16, 96), :], fa[f + 1, pl.ds(16, 96), :]], 1)
            res = dot3(tab, split(rows))
            part[2 * i] = res[:, :LEV]
            part[2 * i + 1] = res[:, LEV:]
            return carry
        lax.fori_loop(0, SPEC // 2, transform, 0)

        def chunk(p):
            return part.at[:, pl.ds(pl.multiple_of(p * ko, 8), ko), :]
        peers(lambda p: to_lon(chunk(p), rsb.at[lon], rssem.at[0], rssem.at[1], p).start())
        rsb[lon] = part[:, pl.ds(pl.multiple_of(lon * ko, 8), ko), :]

    col0 = jnp.broadcast_to(vmix_ref[:, 0:1], (LEV, LEV))
    rowid = lax.broadcasted_iota(jnp.int32, (LEV, LEV), 0)
    both = jnp.concatenate([vmix_ref[...], col0 + jnp.where(rowid == 0, 1.0, 0.0)], 1)
    bhi, blo = split(both)
    vb[0, pl.ds(0, LEV), :] = bhi
    vb[0, pl.ds(LEV, LEV), :] = bhi
    vb[1, pl.ds(0, LEV), :] = blo
    vb[1, pl.ds(LEV, LEV), :] = jnp.zeros_like(blo)

    def levels(x):
        both = jnp.concatenate(split(x), 1)
        res = dot(both, vb[0]) + dot(both, vb[1])
        return x + res[:, :LEV], res[:, LEV:]

    cour = cour_ref[...]
    east = 0.1 - 0.5 * cour
    west = 0.1 + 0.5 * cour
    wv[0] = wave_ref[0]
    wv[1] = wave_ref[1] * cour

    lat_recvs(halo, asem)
    for i in range(HALO):
        fa[40 + i, pl.ds(16, COLS), :] = halo[1, i]

    @pl.when(jnp.logical_not(polar))
    def _():
        for i in range(HALO):
            fa[2 + i, pl.ds(16, COLS), :] = halo[0, i]

    @pl.when(polar)
    def _():
        for i in range(HALO):
            fa[2 + i] = jnp.zeros((WIDE, LEV), f32)
            fb[2 + i] = jnp.zeros((WIDE, LEV), f32)

    def gather_rows(own_of, got):
        mt[...] = jnp.zeros_like(mt)

        def put(m, carry):
            mt[pl.ds(m + 8, 1), :] = own_of(m)
            return carry
        lax.fori_loop(0, ROWS, put, 0)
        for i in range(HALO):
            mt[40 + i:41 + i, :] = got[1, i]

        @pl.when(jnp.logical_not(polar))
        def _():
            for i in range(HALO):
                mt[2 + i:3 + i, :] = got[0, i]
        return mt[...].T

    lat_recvs(coefr, csem)
    fa[48, pl.ds(16, COLS), :] = gather_rows(lambda m: coef_ref[natural(m)], coefr)[:COLS]

    def pack(f, carry):
        sendx[0, f] = fa[f, pl.ds(16 + COLS - 8, 8), :]
        sendx[1, f] = fa[f, pl.ds(16, 8), :]
        return carry
    lax.fori_loop(2, FRAMES, pack, 0)
    zero = jnp.zeros((8, LEV), f32)
    for s in range(2):
        for f in range(2):
            sendx[s, f] = zero
    ahead = lax.rem(lon + 1, nl)
    behind = lax.rem(lon + nl - 1, nl)
    to_east = to_lon(sendx.at[0], recvx.at[0], xsem.at[0], xsem.at[2], ahead)
    to_west = to_lon(sendx.at[1], recvx.at[1], xsem.at[1], xsem.at[3], behind)
    to_east.start()
    to_west.start()

    wait_bytes(seab.at[pl.ds(0, ROWS - rp)], seas.at[1])
    lat_sends(seab, sear, searow)
    lat_recvs(sear, searow)
    st0[...] = jnp.zeros_like(st0)
    st1[...] = jnp.zeros_like(st1)
    st0[pl.ds(Q0, QN), :] = gather_rows(lambda m: seab[natural(m)], sear)[:QN]

    to_east.wait_recv()
    to_west.wait_recv()

    def unpack(f, carry):
        fa[f, pl.ds(8, 8), :] = recvx[0, f]
        fa[f, pl.ds(16 + COLS, 8), :] = recvx[1, f]
        return carry
    lax.fori_loop(2, FRAMES, unpack, 0)
    coeft[...] = fa[48, pl.ds(Q0, QN), :]

    @pl.when(polar)
    def _():
        sa[0] = jnp.zeros((2 * KW, LEV), f32)
        sb[0] = jnp.zeros((2 * KW, LEV), f32)
        wait_bytes(rsb.at[pl.ds(0, nl - 1)], rssem.at[1])

        def add_up(r, carry):
            total = rsb[0, r]
            for d in range(1, nl):
                total = total + rsb[d, r]
            sa[r + 1, pl.ds(pl.multiple_of(lon * ko, 8), ko), :] = total
            return carry
        lax.fori_loop(0, SPEC, add_up, 0)
        mine = sa.at[pl.ds(1, SPEC), pl.ds(pl.multiple_of(lon * ko, 8), ko), :]
        peers(lambda p: to_lon(mine, mine, agsem.at[0], agsem.at[1], p).start())

    first = jnp.where(polar, 5, 0)
    lane_ok = jnp.logical_or(lane >= 8, jnp.logical_not(polar))
    kid = lax.broadcasted_iota(jnp.int32, (KW, LEV), 0)
    klane = lax.broadcasted_iota(jnp.int32, (2 * KW, LEV), 1)
    glane = lax.broadcasted_iota(jnp.int32, (PACK, LEV), 1) // 32

    for t in range(1, STEPS + 1):
        src, dst = (fa, fb) if t % 2 else (fb, fa)
        ssrc, sdst = (sa, sb) if t % 2 else (sb, sa)
        sea, sea_next = (st0, st1) if t % 2 else (st1, st0)

        def grid_rows(i, acc):
            adv = []
            for j in range(4):
                f = 4 * i + 2 + j
                mid = pl.ds(Q0, QN)
                adv.append(0.6 * src[f, mid, :] + 0.1 * (src[f - 1, mid, :] + src[f + 1, mid, :])
                           + east * src[f, pl.ds(Q0 + 1, QN), :] + west * src[f, pl.ds(Q0 - 1, QN), :])
            new, low = levels(jnp.concatenate(adv, 0))
            for j in range(4):
                f = 4 * i + 2 + j
                dst[f, pl.ds(Q0, QN), :] = new[j * QN:(j + 1) * QN]
                acc = jnp.where(lane == f, low[j * QN:(j + 1) * QN], acc)
            return acc
        a0t[...] = lax.fori_loop(first, 11, grid_rows, jnp.zeros((QN, LEV), f32))

        @pl.when(polar)
        def _():
            if t == 1:
                loads[1].wait()
                loads[2].wait()
                wait_bytes(sa.at[pl.ds(1, SPEC), pl.ds(0, ko * (nl - 1)), :], agsem.at[1])
            else:
                wait_bytes(fx.at[t - 2, pl.ds(0, nl - 1)], fxs.at[t - 2, 1])
                got = split(fx[t - 2].reshape(nl * PACK, LEV))
                hat = jnp.zeros((2 * KW, LEV), f32)
                for g in range(4):
                    res = dot3((ct[0, g], ct[1, g]), got)
                    hat = hat + jnp.where(klane // 32 == g, res, 0.0)
                hat = hat + pltpu.roll(hat, 64, 1)
                hat = hat + pltpu.roll(hat, 32, 1)

                def add_flux(r, carry):
                    turned = pltpu.roll(hat, lax.rem(LEV - r, LEV), 1)
                    ssrc[r + 1] = ssrc[r + 1] + jnp.where(klane == 0, 0.5 * turned, 0.0)
                    return carry
                lax.fori_loop(0, SPEC + 1 - t, add_flux, 0)

            def waves(r, acc):
                here, up, down = ssrc[r + 1], ssrc[r], ssrc[r + 2]
                re, im = here[:KW], here[KW:]
                near = 0.1 * (up + down)
                c, s = wv[0], wv[1]
                are = c * re - s * im + near[:KW]
                aim = c * im + s * re + near[KW:]
                cut = jnp.where(r < NPOLE, cut_ref[jnp.where(flip, 2 * NPOLE - 1 - jnp.minimum(r, NPOLE - 1), jnp.minimum(r, NPOLE - 1))], KW)
                keep = kid <= cut
                adv = jnp.concatenate([jnp.where(keep, are, 0.0), jnp.where(keep, aim, 0.0)], 0)
                new, low = levels(adv)
                sdst[r + 1] = new
                return jnp.where(klane == r + 8, low, acc)
            s0t[...] = lax.fori_loop(0, SPEC - t, waves, jnp.zeros((2 * KW, LEV), f32))
            res = dot3((inv[0], inv[1]), split(jnp.concatenate([s0t[...], sdst[NPOLE]], 1)))
            filtered = jnp.logical_and(lane >= 8, lane < 8 + NPOLE)
            a0t[...] = jnp.where(filtered, res[:, :LEV], a0t[...])
            dst[7 + NPOLE, pl.ds(Q0, QN), :] = res[:, LEV:]
            if t == 1:
                wait_bytes(sa.at[pl.ds(1, SPEC), pl.ds(0, ko * (nl - 1)), :], agsem.at[0])

        now = sea[pl.ds(Q0, QN), :]
        flux = coeft[...] * (now - a0t[...])
        fluxt[...] = flux
        around = (pltpu.roll(now, 1, 1) + pltpu.roll(now, LEV - 1, 1)
                  + sea[pl.ds(Q0 - 1, QN), :] + sea[pl.ds(Q0 + 1, QN), :])
        later = now - 0.3 * flux + 0.2 * (around - 4.0 * now)
        sea_next[pl.ds(Q0, QN), :] = jnp.where(lane_ok, later, 0.0)

        if t < STEPS:
            @pl.when(polar)
            def _():
                msg = jnp.zeros((PACK, LEV), f32)
                for g in range(4):
                    turned = pltpu.roll(fluxt[pl.ds(8 + PACK * g, PACK), :], (32 * g - 8) % LEV, 1)
                    msg = jnp.where(glane == g, turned, msg)
                fp[t - 1] = msg
                fx[t - 1, lon] = msg
                peers(lambda p: to_lon(fp.at[t - 1], fx.at[t - 1, lon], fxs.at[t - 1, 0], fxs.at[t - 1, 1], p).start())

        def warm(f, carry):
            turned = pltpu.roll(fluxt[...], LEV - f, 1)
            dst[f, pl.ds(Q0, QN), :] = dst[f, pl.ds(Q0, QN), :] + jnp.where(lane == 0, 0.5 * turned, 0.0)
            return carry
        lax.fori_loop(jnp.where(polar, 23, 2), 46, warm, 0)

    last, slast, sea = fa, sa, st0

    mt[...] = sea[pl.ds(16, LEV), :].T

    def put_row(n, carry):
        seaf[n] = mt[pl.ds(natural(n) + 8, 1), :]
        return carry
    lax.fori_loop(0, ROWS, put_row, 0)
    peers(lambda p: to_lon(seaf.at[pl.ds(rp * p, rp)], seafin.at[lon], fins.at[0], fins.at[1], p).start())

    def own_fin(i, carry):
        seafin[lon, i] = seaf[rp * lon + i]
        return carry
    lax.fori_loop(0, rp, own_fin, 0)

    @pl.when(polar)
    def _():
        tab = (inv[0], inv[1])

        def give(i, carry):
            res = dot3(tab, split(jnp.concatenate([slast[2 * i + 1], slast[2 * i + 2]], 1)))
            for j in range(2):
                turned = pltpu.roll(fluxt[...], LEV - 8 - (2 * i + j), 1)
                value = res[:, j * LEV:(j + 1) * LEV] + jnp.where(lane == 0, 0.5 * turned, 0.0)
                out_ref[natural(2 * i + j)] = value[8:8 + COLS]
            return carry
        lax.fori_loop(0, NPOLE // 2, give, 0)

    def give_grid(m, carry):
        out_ref[natural(m)] = last[m + 8, pl.ds(16, COLS), :]
        return carry
    lax.fori_loop(jnp.where(polar, NPOLE, 0), ROWS, give_grid, 0)

    wait_bytes(seafin.at[pl.ds(0, nl - 1)], fins.at[1])
    seaout_ref[...] = seafin[...]

    wait_bytes(seafin.at[pl.ds(0, nl - 1)], fins.at[0])
    wait_bytes(seab.at[pl.ds(0, ROWS - rp)], seas.at[0])
    lat_sent(halo, asem)
    lat_sent(coefr, csem)
    lat_sent(sear, searow)
    to_east.wait_send()
    to_west.wait_send()

    @pl.when(polar)
    def _():
        wait_bytes(rsb.at[pl.ds(0, nl - 1)], rssem.at[0])
        for t in range(STEPS - 1):
            wait_bytes(fx.at[t, pl.ds(0, nl - 1)], fxs.at[t, 0])


def local(nl, consts, air, sea, land, courant, vmix, cutoffs):
    rp = ROWS // nl
    ko = 2 * KW // nl
    blocks = sea.reshape(rp, nl, COLS)
    wide = jnp.concatenate([jnp.roll(blocks, 1, 1)[:, :, COLS - 8:], blocks, jnp.roll(blocks, -1, 1)[:, :, :8]], 2)
    wide = jnp.pad(wide, ((0, 0), (0, 0), (0, LEV - COLS - 16)))
    seaw = wide.transpose(1, 0, 2)[:, :, None, :]
    coef = jnp.pad(jnp.where(land == 1, 0.5, 0.15).astype(f32), ((0, 0), (0, LEV - COLS)))[:, None, :]
    own, inv, ct, wave = consts
    vm = pl.BlockSpec(memory_space=pltpu.VMEM)
    hbm = pl.BlockSpec(memory_space=pl.ANY)
    dma = pltpu.SemaphoreType.DMA
    v = pltpu.VMEM
    air_out, sea_out = pl.pallas_call(
        functools.partial(kernel, nl),
        out_shape=(jax.ShapeDtypeStruct((ROWS, COLS, LEV), f32),
                   jax.ShapeDtypeStruct((nl, rp, 1, LEV), f32)),
        in_specs=[vm, vm, vm, vm, vm, pl.BlockSpec(memory_space=pltpu.SMEM), hbm, hbm, hbm, vm],
        out_specs=(vm, vm),
        scratch_shapes=[
            v((FRAMES, WIDE, LEV), f32), v((FRAMES, WIDE, LEV), f32),
            v((SPEC + 2, 2 * KW, LEV), f32), v((SPEC + 2, 2 * KW, LEV), f32),
            v((SPEC, 2 * KW, LEV), f32), v((nl, SPEC, ko, LEV), f32),
            v((STEPS - 1, nl, PACK, LEV), f32), v((STEPS - 1, PACK, LEV), f32),
            v((2, HALO, COLS, LEV), f32), v((2, HALO, 1, LEV), f32), v((2, HALO, 1, LEV), f32),
            v((ROWS, 1, LEV), f32), v((ROWS, 1, LEV), f32), v((nl, rp, 1, LEV), f32),
            v((2, FRAMES, 8, LEV), f32), v((2, FRAMES, 8, LEV), f32),
            v((2, 2 * KW, 96), bf16), v((2, QN, 2 * KW), bf16), v((2, 4, 2 * KW, nl * PACK), bf16),
            v((2, 2 * LEV, 2 * LEV), bf16), v((LEV, LEV), f32),
            v((QN, LEV), f32), v((QN, LEV), f32), v((144, LEV), f32), v((144, LEV), f32),
            v((QN, LEV), f32), v((2 * KW, LEV), f32), v((2, KW, LEV), f32),
            dma((3,)), dma((4,)), dma((4,)), dma((2,)), dma((4,)), dma((4,)), dma((2,)), dma((2,)),
            dma((STEPS - 1, 2)), dma((2,)),
        ],
        compiler_params=pltpu.CompilerParams(
            collective_id=0, has_side_effects=True, vmem_limit_bytes=56 * 1024 * 1024),
    )(air, seaw, coef, courant.reshape(1, LEV), vmix, cutoffs, own, inv, ct, wave)
    sea_out = sea_out[:, :, 0, :COLS].transpose(1, 0, 2).reshape(rp, nl * COLS)
    return air_out, sea_out


def solution(mesh):
    nl = mesh.shape["lon"]
    consts = tuple(jnp.asarray(x) for x in tables(nl))
    placed = (P("lat", "lon", None), P(("lat", "lon"), None), P("lat", "lon"), P(), P(), P())

    def run(*args):
        return jax.shard_map(
            functools.partial(local, nl),
            mesh=mesh,
            in_specs=((P(),) * 4,) + placed,
            out_specs=(P("lat", "lon", None), P(("lat", "lon"), None)),
            check_vma=False,
        )(consts, *args)

    return run
```

```python
import functools

import jax
import jax.numpy as jnp
import ml_dtypes
import numpy as np
from jax import lax
from jax.experimental import pallas as pl
from jax.experimental.pallas import tpu as pltpu
from jax.sharding import PartitionSpec as P

STEPS = 6
NPOLE = 16
ROWS = 32
COLS = 90
KW = 128
LEV = 128
HALO = 6
FRAMES = 49
WIDE = 120
Q0, QN = 8, 104
SPEC = NPOLE + HALO
GROUPS, GW = 6, 16
STARTS = (0, 15, 30, 45, 60, 74)

f32, bf16 = jnp.float32, jnp.bfloat16
MESH = pl.DeviceIdType.MESH


def split(x):
    hi = x.astype(bf16)
    return hi, (x - hi.astype(f32)).astype(bf16)


def dot(a, b):
    return jnp.dot(a, b, preferred_element_type=f32)


def dot3(a, b):
    return dot(a[0], b[0]) + dot(a[1], b[0]) + dot(a[0], b[1])


def np_split(x):
    x = x.astype(np.float32)
    hi = x.astype(ml_dtypes.bfloat16)
    lo = (x - hi.astype(np.float32)).astype(ml_dtypes.bfloat16)
    return np.stack([hi, lo])


def tables(nl):
    nlon = nl * COLS
    kq = KW // nl
    k = (np.arange(nl)[:, None, None] * kq + np.arange(kq)[None, None, :]) * np.ones((1, 2, 1), int)
    sine = np.broadcast_to(np.arange(2)[None, :, None], k.shape).reshape(-1)
    k = k.reshape(-1)

    def fwd(c):
        ang = (c[..., None] * k % nlon) * (2.0 * np.pi / nlon)
        return np.where(sine == 0, np.cos(ang), np.sin(ang))

    d = np.arange(nl)[:, None]
    q = np.arange(QN)[None]
    weight = np.where(k == 0, 1.0, 2.0) / nlon
    inv = np.moveaxis(np_split(fwd((d * COLS + q - 8) % nlon) * weight), 0, 1)
    packed = []
    for g in range(GROUPS):
        c = STARTS[g] + np.arange(GW)[None]
        ours = np.logical_and(c >= g * 15, c < g * 15 + 15)
        packed.append(np.where(ours[..., None], fwd(d * COLS + c), 0.0).reshape(nl * GW, 2 * KW).T)
    fold = np.zeros((LEV, 2 * LEV))
    for g in range(GROUPS):
        for r in range(SPEC - 1):
            fold[21 * g + r, r + 8] = 0.5
            for near in (r - 1, r + 1):
                if near >= 0:
                    fold[21 * g + r, LEV + near + 8] = 0.5
    fold = np.concatenate([fold, fold]).astype(ml_dtypes.bfloat16)
    step = 2.0 * np.pi / nlon
    wave = np.stack([0.6 + 0.2 * np.cos(k * step), np.where(sine == 0, -1.0, 1.0) * np.sin(k * step)])
    wave = np.broadcast_to(wave[:, :, None], (2, 2 * KW, LEV)).astype(np.float32)
    return inv, np_split(np.concatenate(packed, 0)), fold, wave


def kernel(nl, a_ref, seaw_ref, coef_ref, cour_ref, vmix_ref, cut_ref, inv_hbm, ct_hbm, fold_ref,
           wave_ref, out_ref, seaout_ref, fa, fb, sa, sb, rowb, spec, ex, ep, ag, halo, coefr, sear,
           seab, seaf, seafin, sendx, recvx, inv, ct, vb, mt, a0t, coeft, st0, st1, fluxt,
           at, keept, tsem, asem, csem, seas, searow, xsem, rows, kss, exs, agsem, fins):
    lat, lon = lax.axis_index("lat"), lax.axis_index("lon")
    polar = jnp.logical_or(lat == 0, lat == 3)
    flip = lat == 3
    kq = KW // nl
    ko = 2 * kq
    rp = ROWS // nl
    half = nl // 2
    turn = lax.rem(lon, half) * 2 + lon // half
    lane = lax.broadcasted_iota(jnp.int32, (QN, LEV), 1)

    def natural(m):
        return jnp.where(flip, ROWS - 1 - m, m)

    def peers(body):
        def one(i, carry):
            body(lax.rem(lon + i, nl))
            return carry
        lax.fori_loop(1, nl, one, 0)

    def wait_bytes(ref, sem):
        pltpu.make_async_copy(ref, ref, sem).wait()

    def to_lon(src, dst, ssem, rsem, peer):
        return pltpu.make_async_remote_copy(src, dst, ssem, rsem, device_id={"lon": peer},
                                            device_id_type=MESH)

    loads = [
        pltpu.make_async_copy(inv_hbm.at[lon], inv, tsem.at[0]),
        pltpu.make_async_copy(ct_hbm, ct, tsem.at[1]),
    ]

    @pl.when(polar)
    def _():
        for load in loads:
            load.start()

    barrier = pltpu.get_barrier_semaphore()
    peers(lambda p: pl.semaphore_signal(barrier, inc=1, device_id={"lon": p}, device_id_type=MESH))

    @pl.when(lat < 3)
    def _():
        pl.semaphore_signal(barrier, inc=1, device_id={"lat": lat + 1}, device_id_type=MESH)

    @pl.when(lat > 0)
    def _():
        pl.semaphore_signal(barrier, inc=1, device_id={"lat": lat - 1}, device_id_type=MESH)

    pl.semaphore_wait(barrier, nl - 1 + jnp.where(polar, 1, 2))

    side = jnp.where(lat == 2, 1, 0)

    def lat_sends(src_ref, dst_ref, sems):
        def make(src, s, i, which, to):
            return pltpu.make_async_remote_copy(
                src_ref.at[src], dst_ref.at[s, i], sems.at[which], sems.at[2 + s],
                device_id={"lat": to}, device_id_type=MESH)

        @pl.when(lat < 3)
        def _():
            for i in range(HALO):
                make(jnp.where(lat == 2, ROWS - 1 - i, ROWS - HALO + i), side, i, 0, lat + 1).start()

        @pl.when(lat > 0)
        def _():
            for i in range(HALO):
                make(i, 1, i, 1, lat - 1).start()

    def lat_recvs(dst_ref, sems):
        wait_bytes(dst_ref.at[1], sems.at[3])

        @pl.when(jnp.logical_not(polar))
        def _():
            wait_bytes(dst_ref.at[0], sems.at[2])

    def lat_sent(dst_ref, sems):
        @pl.when(lat < 3)
        def _():
            wait_bytes(dst_ref.at[0], sems.at[0])

        @pl.when(lat > 0)
        def _():
            wait_bytes(dst_ref.at[0], sems.at[1])

    def owner(r):
        return (r % nl) % 2 * half + r % nl // 2

    @pl.when(polar)
    def _():
        for r in range(SPEC):
            @pl.when(lon != owner(r))
            def _():
                to_lon(a_ref.at[natural(r)], rowb.at[r // nl, lon], rows.at[0], rows.at[1 + r // nl], owner(r)).start()

    peers(lambda p: to_lon(seaw_ref.at[p], seab.at[pl.ds(rp * lon, rp)], seas.at[0], seas.at[1], p).start())
    lat_sends(coef_ref, coefr, csem)
    lat_sends(a_ref, halo, asem)

    @pl.when(polar)
    def _():
        for r in range(SPEC):
            @pl.when(lon == owner(r))
            def _():
                rowb[r // nl, lon] = a_ref[natural(r)]

    def own_sea(i, carry):
        seab[rp * lon + i] = seaw_ref[lon, i]
        return carry
    lax.fori_loop(0, rp, own_sea, 0)

    def clear(f, carry):
        z = jnp.zeros((8, LEV), f32)
        fa[f, pl.ds(0, 8), :] = z
        fa[f, pl.ds(WIDE - 16, 8), :] = z
        fa[f, pl.ds(WIDE - 8, 8), :] = z
        fb[f, pl.ds(0, 8), :] = z
        fb[f, pl.ds(WIDE - 8, 8), :] = z
        return carry
    lax.fori_loop(0, FRAMES, clear, 0)
    for f in (0, 1, 46, 47):
        fa[f] = jnp.zeros((WIDE, LEV), f32)
        fb[f] = jnp.zeros((WIDE, LEV), f32)
    fa[48] = jnp.zeros((WIDE, LEV), f32)
    fb[48] = jnp.zeros((WIDE, LEV), f32)

    def fill(m, carry):
        fa[m + 8, pl.ds(16, COLS), :] = a_ref[natural(m)]
        return carry
    lax.fori_loop(0, ROWS, fill, 0)

    col0 = jnp.broadcast_to(vmix_ref[:, 0:1], (LEV, LEV))
    rowid = lax.broadcasted_iota(jnp.int32, (LEV, LEV), 0)
    both = jnp.concatenate([vmix_ref[...], col0 + jnp.where(rowid == 0, 1.0, 0.0)], 1)
    bhi, blo = split(both)
    vb[0, pl.ds(0, LEV), :] = bhi
    vb[0, pl.ds(LEV, LEV), :] = bhi
    vb[1, pl.ds(0, LEV), :] = blo
    vb[1, pl.ds(LEV, LEV), :] = jnp.zeros_like(blo)

    def levels(x):
        both = jnp.concatenate(split(x), 1)
        res = dot(both, vb[0]) + dot(both, vb[1])
        return x + res[:, :LEV], res[:, LEV:]

    cour = cour_ref[...]
    east = 0.1 - 0.5 * cour
    west = 0.1 + 0.5 * cour
    lane1 = lax.broadcasted_iota(jnp.int32, (1, LEV), 1)
    vrow0 = vmix_ref[0:1, :] + jnp.where(lane1 == 0, 1.0, 0.0)
    half0 = jnp.where(lane1 == 0, 0.5, 0.0)
    kown = lon * kq + lax.rem(lax.broadcasted_iota(jnp.int32, (ko, LEV), 0), kq)
    olane = lax.broadcasted_iota(jnp.int32, (ko, LEV), 1)
    krow = lax.broadcasted_iota(jnp.int32, (2 * KW, LEV), 0)
    klane = lax.broadcasted_iota(jnp.int32, (2 * KW, LEV), 1)

    def swap(x, rowid):
        return jnp.where(lax.rem(rowid, ko) < kq, pltpu.roll(x, x.shape[0] - kq, 0), pltpu.roll(x, kq, 0))

    def cutoff(r):
        return cut_ref[jnp.where(flip, 2 * NPOLE - 1 - r, r)]

    mine = pl.ds(pl.multiple_of(lon * ko, 8), ko)

    @pl.when(polar)
    def _():
        cuts = jnp.full((1, LEV), KW, jnp.int32)
        for r in range(NPOLE):
            cuts = jnp.where(lane1 == r + 8, cutoff(r), cuts)
        kid = krow // ko * kq + lax.rem(krow, kq)
        keept[...] = jnp.where(kid <= cuts, 1.0, 0.0)
        for buf in (sa, sb):
            buf[0] = jnp.zeros((ko, LEV), f32)
            buf[SPEC + 1] = jnp.zeros((ko, LEV), f32)

    lat_recvs(halo, asem)
    for i in range(HALO):
        fa[40 + i, pl.ds(16, COLS), :] = halo[1, i]

    @pl.when(jnp.logical_not(polar))
    def _():
        for i in range(HALO):
            fa[2 + i, pl.ds(16, COLS), :] = halo[0, i]

    @pl.when(polar)
    def _():
        for i in range(HALO):
            fa[2 + i] = jnp.zeros((WIDE, LEV), f32)
            fb[2 + i] = jnp.zeros((WIDE, LEV), f32)

    def gather_rows(own_of, got):
        mt[...] = jnp.zeros_like(mt)

        def put(m, carry):
            mt[pl.ds(m + 8, 1), :] = own_of(m)
            return carry
        lax.fori_loop(0, ROWS, put, 0)
        for i in range(HALO):
            mt[40 + i:41 + i, :] = got[1, i]

        @pl.when(jnp.logical_not(polar))
        def _():
            for i in range(HALO):
                mt[2 + i:3 + i, :] = got[0, i]
        return mt[...].T

    lat_recvs(coefr, csem)
    fa[48, pl.ds(16, COLS), :] = gather_rows(lambda m: coef_ref[natural(m)], coefr)[:COLS]

    def pack(f, carry):
        sendx[0, f] = fa[f, pl.ds(16 + COLS - 8, 8), :]
        sendx[1, f] = fa[f, pl.ds(16, 8), :]
        return carry
    lax.fori_loop(2, FRAMES, pack, 0)
    zero = jnp.zeros((8, LEV), f32)
    for s in range(2):
        for f in range(2):
            sendx[s, f] = zero
    ahead = lax.rem(lon + 1, nl)
    behind = lax.rem(lon + nl - 1, nl)
    to_east = to_lon(sendx.at[0], recvx.at[0], xsem.at[0], xsem.at[2], ahead)
    to_west = to_lon(sendx.at[1], recvx.at[1], xsem.at[1], xsem.at[3], behind)
    to_east.start()
    to_west.start()

    wait_bytes(seab.at[pl.ds(0, ROWS - rp)], seas.at[1])
    lat_sends(seab, sear, searow)

    @pl.when(polar)
    def _():
        loads[0].wait()
        loads[1].wait()
        for slot in range(-(-SPEC // nl)):
            r = slot * nl + turn

            @pl.when(r < SPEC)
            def _():
                wait_bytes(rowb.at[slot, pl.ds(0, nl - 1)], rows.at[1 + slot])
                acc = jnp.zeros((2 * KW, LEV), f32)
                for g in range(GROUPS):
                    cols = rowb[slot, :, pl.ds(STARTS[g], GW), :].reshape(nl * GW, LEV)
                    tab = (ct[0, pl.ds(2 * KW * g, 2 * KW), :], ct[1, pl.ds(2 * KW * g, 2 * KW), :])
                    acc = acc + dot3(tab, split(cols))
                spec[slot] = acc

                def chunk(p):
                    return spec.at[slot, pl.ds(pl.multiple_of(p * ko, 8), ko)]
                peers(lambda p: to_lon(chunk(p), sa.at[r + 1], kss.at[0], kss.at[1], p).start())
                sa[r + 1] = spec[slot, mine, :]

    lat_recvs(sear, searow)
    st0[...] = jnp.zeros_like(st0)
    st1[...] = jnp.zeros_like(st1)
    st0[pl.ds(Q0, QN), :] = gather_rows(lambda m: seab[natural(m)], sear)[:QN]

    to_east.wait_recv()
    to_west.wait_recv()

    def unpack(f, carry):
        fa[f, pl.ds(8, 8), :] = recvx[0, f]
        fa[f, pl.ds(16 + COLS, 8), :] = recvx[1, f]
        return carry
    lax.fori_loop(2, FRAMES, unpack, 0)
    coeft[...] = fa[48, pl.ds(Q0, QN), :]

    def evolve(t, src, dst):
        wc = wave_ref[0, mine, :]
        ws = wave_ref[1, mine, :] * cour
        adv = []
        for r in range(SPEC - 1 - t):
            here = src[r + 1]
            x = wc * here + ws * swap(here, lax.broadcasted_iota(jnp.int32, (ko, LEV), 0)) + 0.1 * (src[r] + src[r + 2])
            adv.append(jnp.where(kown <= cutoff(r), x, 0.0) if r < NPOLE else x)
        new, low = levels(jnp.concatenate(adv, 0))
        level0 = jnp.zeros((ko, LEV), f32)
        for r in range(SPEC - 1 - t):
            dst[r + 1] = new[r * ko:(r + 1) * ko]
            if r < NPOLE:
                level0 = jnp.where(olane == r + 8, low[r * ko:(r + 1) * ko], level0)
        ep[t, pl.ds(0, ko), :] = level0
        ep[t, pl.ds(ko, ko), :] = new[(NPOLE - 1) * ko:NPOLE * ko]

    def message(t, height):
        part = pl.ds(0, height)
        ex[t, lon, part, :] = ep[t, part, :]
        peers(lambda p: to_lon(ep.at[t, part], ex.at[t, lon, part], exs.at[t, 0], exs.at[t, 1], p).start())

    def message_wait(t, height, which):
        wait_bytes(ex.at[t, pl.ds(0, nl - 1), pl.ds(0, height)], exs.at[t, which])

    def height(t):
        return 2 * ko + (GW if t else 0)

    @pl.when(polar)
    def _():
        extra = turn < SPEC % nl

        @pl.when(extra)
        def _():
            wait_bytes(sa.at[pl.ds(1, SPEC - SPEC // nl - 1)], kss.at[1])

        @pl.when(jnp.logical_not(extra))
        def _():
            wait_bytes(sa.at[pl.ds(1, SPEC - SPEC // nl)], kss.at[1])
        evolve(0, sa, sb)
        message(0, height(0))

    lane_ok = jnp.logical_or(lane >= 8, jnp.logical_not(polar))
    glane = lax.broadcasted_iota(jnp.int32, (GW, LEV), 1) // 21

    for t in range(1, STEPS + 1):
        src, dst = (fa, fb) if t % 2 else (fb, fa)
        sprev, snow = (sa, sb) if t % 2 else (sb, sa)
        sea, sea_next = (st0, st1) if t % 2 else (st1, st0)
        first = jnp.where(polar, 8 + NPOLE, 2 + t)
        count = jnp.where(polar, -(-(22 - t) // 4), -(-(44 - 2 * t) // 4))

        def grid_rows(i, acc):
            adv = []
            for j in range(4):
                f = first + 4 * i + j
                mid = pl.ds(Q0, QN)
                adv.append(0.6 * src[f, mid, :] + 0.1 * (src[f - 1, mid, :] + src[f + 1, mid, :])
                           + east * src[f, pl.ds(Q0 + 1, QN), :] + west * src[f, pl.ds(Q0 - 1, QN), :])
            new, low = levels(jnp.concatenate(adv, 0))
            for j in range(4):
                f = first + 4 * i + j
                dst[f, pl.ds(Q0, QN), :] = new[j * QN:(j + 1) * QN]
                acc = jnp.where(lane == f, low[j * QN:(j + 1) * QN], acc)
            return acc
        a0t[...] = lax.fori_loop(0, count, grid_rows, jnp.zeros((QN, LEV), f32))

        @pl.when(polar)
        def _():
            message_wait(t - 1, height(t - 1), 1)
            level0 = ex[t - 1, :, pl.ds(0, ko), :].reshape(2 * KW, LEV)
            edge = ex[t - 1, :, pl.ds(ko, ko), :].reshape(2 * KW, LEV)
            if t > 1:
                got = split(ex[t - 1, :, pl.ds(2 * ko, GW), :].reshape(nl * GW, LEV))
                res = jnp.zeros((2 * KW, LEV), f32)
                for g in range(GROUPS):
                    tab = (ct[0, pl.ds(2 * KW * g, 2 * KW), :], ct[1, pl.ds(2 * KW * g, 2 * KW), :])
                    res = jnp.where(klane // 21 == g, dot3(tab, got), res)
                hats = dot(jnp.concatenate(split(res), 1), fold_ref[...])
                hat, near = hats[:, :LEV], hats[:, LEV:]
                add = wave_ref[0] * hat + wave_ref[1] * cour[:, 0:1] * swap(hat, krow) + 0.1 * near
                add = add * keept[...]
                level0 = level0 + vrow0[:, 0:1] * add
                if t < STEPS:
                    at[...] = add
                    edge = edge + add[:, 7 + NPOLE:8 + NPOLE] * vrow0
                    own = at[mine, :]
                    for r in range(SPEC - t):
                        snow[r + 1] = snow[r + 1] + own[:, r + 8:r + 9] * vrow0
                else:
                    edge = add
            res = dot3((inv[0], inv[1]), split(jnp.concatenate([level0, edge], 1)))
            filtered = jnp.logical_and(lane >= 8, lane < 8 + NPOLE)
            a0t[...] = jnp.where(filtered, res[:, :LEV], a0t[...])
            if t < STEPS:
                dst[7 + NPOLE, pl.ds(Q0, QN), :] = res[:, LEV:]
                evolve(t, snow, sprev)
            else:
                at[pl.ds(0, QN), :] = res[:, LEV:]

        now = sea[pl.ds(Q0, QN), :]
        flux = coeft[...] * (now - a0t[...])
        fluxt[...] = flux
        around = (pltpu.roll(now, 1, 1) + pltpu.roll(now, LEV - 1, 1)
                  + sea[pl.ds(Q0 - 1, QN), :] + sea[pl.ds(Q0 + 1, QN), :])
        later = now - 0.3 * flux + 0.2 * (around - 4.0 * now)
        sea_next[pl.ds(Q0, QN), :] = jnp.where(lane_ok, later, 0.0)

        if t < STEPS:
            @pl.when(polar)
            def _():
                msg = jnp.zeros((GW, LEV), f32)
                for g in range(GROUPS):
                    turned = pltpu.roll(fluxt[pl.ds(8 + STARTS[g], GW), :], (21 * g - 8) % LEV, 1)
                    msg = jnp.where(glane == g, turned, msg)
                ep[t, pl.ds(2 * ko, GW), :] = msg
                message(t, height(t))
                if t == STEPS - 1:
                    whole = sprev.at[pl.ds(1, NPOLE)]
                    peers(lambda p: to_lon(whole, ag.at[lon], agsem.at[0], agsem.at[1], p).start())
                    ag[lon] = sprev[pl.ds(1, NPOLE)]

        def warm(f):
            dst[f, pl.ds(Q0, QN), :] = dst[f, pl.ds(Q0, QN), :] + flux[:, f:f + 1] * half0

        @pl.when(jnp.logical_not(polar))
        def _():
            for f in range(2 + t, 7 + NPOLE):
                warm(f)
        for f in range(7 + NPOLE, 46 - t):
            warm(f)

    last, sea = fa, st0

    mt[...] = sea[pl.ds(16, LEV), :].T

    def put_row(n, carry):
        seaf[n] = mt[pl.ds(natural(n) + 8, 1), :]
        return carry
    lax.fori_loop(0, ROWS, put_row, 0)
    peers(lambda p: to_lon(seaf.at[pl.ds(rp * p, rp)], seafin.at[lon], fins.at[0], fins.at[1], p).start())

    def own_fin(i, carry):
        seafin[lon, i] = seaf[rp * lon + i]
        return carry
    lax.fori_loop(0, rp, own_fin, 0)

    def give_grid(m, carry):
        out_ref[natural(m)] = last[m + 8, pl.ds(16, COLS), :]
        return carry
    lax.fori_loop(jnp.where(polar, NPOLE, 0), ROWS, give_grid, 0)

    @pl.when(polar)
    def _():
        wait_bytes(ag.at[pl.ds(0, nl - 1)], agsem.at[1])
        tab = (inv[0], inv[1])
        for i in range(NPOLE // 2):
            pair = jnp.concatenate([ag[:, 2 * i].reshape(2 * KW, LEV), ag[:, 2 * i + 1].reshape(2 * KW, LEV)], 1)
            res = dot3(tab, split(pair))
            for j in range(2):
                r = 2 * i + j
                value = (res[:, j * LEV:(j + 1) * LEV] + at[pl.ds(0, QN), r + 8:r + 9] * vrow0
                         + fluxt[:, r + 8:r + 9] * half0)
                out_ref[natural(r)] = value[8:8 + COLS]

    wait_bytes(seafin.at[pl.ds(0, nl - 1)], fins.at[1])
    seaout_ref[...] = seafin[...]

    wait_bytes(seafin.at[pl.ds(0, nl - 1)], fins.at[0])
    wait_bytes(seab.at[pl.ds(0, ROWS - rp)], seas.at[0])
    lat_sent(halo, asem)
    lat_sent(coefr, csem)
    lat_sent(sear, searow)
    to_east.wait_send()
    to_west.wait_send()

    @pl.when(polar)
    def _():
        for r in range(SPEC):
            @pl.when(lon != owner(r))
            def _():
                wait_bytes(a_ref.at[0], rows.at[0])
        for slot in range(-(-SPEC // nl)):
            @pl.when(slot * nl + turn < SPEC)
            def _():
                wait_bytes(spec.at[slot, pl.ds(0, (nl - 1) * ko)], kss.at[0])
        for t in range(STEPS):
            message_wait(t, height(t), 0)
        wait_bytes(ag.at[pl.ds(0, nl - 1)], agsem.at[0])


def local(nl, consts, air, sea, land, courant, vmix, cutoffs):
    rp = ROWS // nl
    ko = 2 * KW // nl
    blocks = sea.reshape(rp, nl, COLS)
    wide = jnp.concatenate([jnp.roll(blocks, 1, 1)[:, :, COLS - 8:], blocks, jnp.roll(blocks, -1, 1)[:, :, :8]], 2)
    wide = jnp.pad(wide, ((0, 0), (0, 0), (0, LEV - COLS - 16)))
    seaw = wide.transpose(1, 0, 2)[:, :, None, :]
    coef = jnp.pad(jnp.where(land == 1, 0.5, 0.15).astype(f32), ((0, 0), (0, LEV - COLS)))[:, None, :]
    inv, ct, fold, wave = consts
    slots = -(-SPEC // nl)
    vm = pl.BlockSpec(memory_space=pltpu.VMEM)
    hbm = pl.BlockSpec(memory_space=pl.ANY)
    dma = pltpu.SemaphoreType.DMA
    v = pltpu.VMEM
    air_out, sea_out = pl.pallas_call(
        functools.partial(kernel, nl),
        out_shape=(jax.ShapeDtypeStruct((ROWS, COLS, LEV), f32),
                   jax.ShapeDtypeStruct((nl, rp, 1, LEV), f32)),
        in_specs=[vm, vm, vm, vm, vm, pl.BlockSpec(memory_space=pltpu.SMEM), hbm, hbm, vm, vm],
        out_specs=(vm, vm),
        scratch_shapes=[
            v((FRAMES, WIDE, LEV), f32), v((FRAMES, WIDE, LEV), f32),
            v((SPEC + 2, ko, LEV), f32), v((SPEC + 2, ko, LEV), f32),
            v((slots, nl, COLS, LEV), f32), v((slots, 2 * KW, LEV), f32),
            v((STEPS, nl, 2 * ko + GW, LEV), f32), v((STEPS, 2 * ko + GW, LEV), f32),
            v((nl, NPOLE, ko, LEV), f32),
            v((2, HALO, COLS, LEV), f32), v((2, HALO, 1, LEV), f32), v((2, HALO, 1, LEV), f32),
            v((ROWS, 1, LEV), f32), v((ROWS, 1, LEV), f32), v((nl, rp, 1, LEV), f32),
            v((2, FRAMES, 8, LEV), f32), v((2, FRAMES, 8, LEV), f32),
            v((2, QN, 2 * KW), bf16), v((2, GROUPS * 2 * KW, nl * GW), bf16),
            v((2, 2 * LEV, 2 * LEV), bf16), v((LEV, LEV), f32),
            v((QN, LEV), f32), v((QN, LEV), f32), v((144, LEV), f32), v((144, LEV), f32),
            v((QN, LEV), f32), v((2 * KW, LEV), f32), v((2 * KW, LEV), f32),
            dma((2,)), dma((4,)), dma((4,)), dma((2,)), dma((4,)), dma((4,)), dma((1 + slots,)), dma((2,)),
            dma((STEPS, 2)), dma((2,)), dma((2,)),
        ],
        compiler_params=pltpu.CompilerParams(
            collective_id=0, has_side_effects=True, vmem_limit_bytes=56 * 1024 * 1024),
    )(air, seaw, coef, courant.reshape(1, LEV), vmix, cutoffs, inv, ct, fold, wave)
    sea_out = sea_out[:, :, 0, :COLS].transpose(1, 0, 2).reshape(rp, nl * COLS)
    return air_out, sea_out


def solution(mesh):
    nl = mesh.shape["lon"]
    consts = tuple(jnp.asarray(x) for x in tables(nl))
    placed = (P("lat", "lon", None), P(("lat", "lon"), None), P("lat", "lon"), P(), P(), P())

    def run(*args):
        return jax.shard_map(
            functools.partial(local, nl),
            mesh=mesh,
            in_specs=((P(),) * 4,) + placed,
            out_specs=(P("lat", "lon", None), P(("lat", "lon"), None)),
            check_vma=False,
        )(consts, *args)

    return run
```

```python
import functools

import jax
import jax.numpy as jnp
import ml_dtypes
import numpy as np
from jax import lax
from jax.experimental import pallas as pl
from jax.experimental.pallas import tpu as pltpu
from jax.sharding import PartitionSpec as P

STEPS = 6
NPOLE = 16
ROWS = 32
COLS = 90
KW = 128
LEV = 128
HALO = 6
FRAMES = 49
WIDE = 120
Q0, QN = 8, 104
SPEC = NPOLE + HALO
GROUPS, GW = 6, 16
STARTS = (0, 15, 30, 45, 60, 74)

f32, bf16 = jnp.float32, jnp.bfloat16
MESH = pl.DeviceIdType.MESH


def split(x):
    hi = x.astype(bf16)
    return hi, (x - hi.astype(f32)).astype(bf16)


def dot(a, b):
    return jnp.dot(a, b, preferred_element_type=f32)


def dot3(a, b):
    return dot(a[0], b[0]) + dot(a[1], b[0]) + dot(a[0], b[1])


def dot3n(a, b):
    n = b[0].shape[1]
    both = dot(a[0], jnp.concatenate(b, 1))
    return both[:, :n] + both[:, n:] + dot(a[1], b[0])


def np_split(x):
    x = x.astype(np.float32)
    hi = x.astype(ml_dtypes.bfloat16)
    lo = (x - hi.astype(np.float32)).astype(ml_dtypes.bfloat16)
    return np.stack([hi, lo])


def tables(nl):
    nlon = nl * COLS
    kq = KW // nl
    k = (np.arange(nl)[:, None, None] * kq + np.arange(kq)[None, None, :]) * np.ones((1, 2, 1), int)
    sine = np.broadcast_to(np.arange(2)[None, :, None], k.shape).reshape(-1)
    k = k.reshape(-1)

    def fwd(c):
        ang = (c[..., None] * k % nlon) * (2.0 * np.pi / nlon)
        return np.where(sine == 0, np.cos(ang), np.sin(ang))

    d = np.arange(nl)[:, None]
    q = np.arange(QN)[None]
    weight = np.where(k == 0, 1.0, 2.0) / nlon
    inv = np.moveaxis(np_split(fwd((d * COLS + q - 8) % nlon) * weight), 0, 1)
    everywhere = np_split(fwd(np.arange(nl * COLS).reshape(nl, COLS)) * weight)
    packed = []
    for g in range(GROUPS):
        c = STARTS[g] + np.arange(GW)[None]
        ours = np.logical_and(c >= g * 15, c < g * 15 + 15)
        packed.append(np.where(ours[..., None], fwd(d * COLS + c), 0.0).reshape(nl * GW, 2 * KW).T)
    fold = np.zeros((LEV, 2 * LEV))
    for g in range(GROUPS):
        for r in range(SPEC - 1):
            fold[21 * g + r, r + 8] = 0.5
            for near in (r - 1, r + 1):
                if near >= 0:
                    fold[21 * g + r, LEV + near + 8] = 0.5
    fold = np.concatenate([fold, fold]).astype(ml_dtypes.bfloat16)
    step = 2.0 * np.pi / nlon
    wave = np.stack([0.6 + 0.2 * np.cos(k * step), np.where(sine == 0, -1.0, 1.0) * np.sin(k * step)])
    wave = np.broadcast_to(wave[:, :, None], (2, 2 * KW, LEV)).astype(np.float32)
    return inv, everywhere, np_split(np.concatenate(packed, 0)), fold, wave


def kernel(nl, a_ref, seaw_ref, coef_ref, cour_ref, vmix_ref, cut_ref, inv_hbm, all_hbm, ct_hbm, fold_ref,
           wave_ref, out_ref, seaout_ref, fa, fb, sa, sb, rowb, spec, fx, fp, ex, ep, rs6, stage, fin, xs, xr, halo, coefr, sear,
           seab, seaf, seafin, sendx, recvx, inv, inva, ct, vb, mt, a0t, coeft, st0, st1, fluxt,
           at, keept, tsem, asem, csem, seas, searow, xsem, rows, kss, fxs, exs, r6, fsem, xss, fins):
    lat, lon = lax.axis_index("lat"), lax.axis_index("lon")
    polar = jnp.logical_or(lat == 0, lat == 3)
    flip = lat == 3
    kq = KW // nl
    ko = 2 * kq
    rp = ROWS // nl
    half = nl // 2
    turn = lax.rem(lon, half) * 2 + lon // half
    lane = lax.broadcasted_iota(jnp.int32, (QN, LEV), 1)

    def natural(m):
        return jnp.where(flip, ROWS - 1 - m, m)

    def peers(body):
        def one(i, carry):
            body(lax.rem(lon + i, nl))
            return carry
        lax.fori_loop(1, nl, one, 0)

    def wait_bytes(ref, sem):
        pltpu.make_async_copy(ref, ref, sem).wait()

    def to_lon(src, dst, ssem, rsem, peer):
        return pltpu.make_async_remote_copy(src, dst, ssem, rsem, device_id={"lon": peer},
                                            device_id_type=MESH)

    loads = [
        pltpu.make_async_copy(inv_hbm.at[lon], inv, tsem.at[0]),
        pltpu.make_async_copy(ct_hbm, ct, tsem.at[1]),
        pltpu.make_async_copy(all_hbm, inva, tsem.at[2]),
    ]

    @pl.when(polar)
    def _():
        for load in loads:
            load.start()

    barrier = pltpu.get_barrier_semaphore()
    peers(lambda p: pl.semaphore_signal(barrier, inc=1, device_id={"lon": p}, device_id_type=MESH))

    @pl.when(lat < 3)
    def _():
        pl.semaphore_signal(barrier, inc=1, device_id={"lat": lat + 1}, device_id_type=MESH)

    @pl.when(lat > 0)
    def _():
        pl.semaphore_signal(barrier, inc=1, device_id={"lat": lat - 1}, device_id_type=MESH)

    pl.semaphore_wait(barrier, nl - 1 + jnp.where(polar, 1, 2))

    side = jnp.where(lat == 2, 1, 0)

    def lat_sends(src_ref, dst_ref, sems):
        def make(src, s, i, which, to):
            return pltpu.make_async_remote_copy(
                src_ref.at[src], dst_ref.at[s, i], sems.at[which], sems.at[2 + s],
                device_id={"lat": to}, device_id_type=MESH)

        @pl.when(lat < 3)
        def _():
            for i in range(HALO):
                make(jnp.where(lat == 2, ROWS - 1 - i, ROWS - HALO + i), side, i, 0, lat + 1).start()

        @pl.when(lat > 0)
        def _():
            for i in range(HALO):
                make(i, 1, i, 1, lat - 1).start()

    def lat_recvs(dst_ref, sems):
        wait_bytes(dst_ref.at[1], sems.at[3])

        @pl.when(jnp.logical_not(polar))
        def _():
            wait_bytes(dst_ref.at[0], sems.at[2])

    def lat_sent(dst_ref, sems):
        @pl.when(lat < 3)
        def _():
            wait_bytes(dst_ref.at[0], sems.at[0])

        @pl.when(lat > 0)
        def _():
            wait_bytes(dst_ref.at[0], sems.at[1])

    def owner(r):
        return (r % nl) % 2 * half + r % nl // 2

    @pl.when(polar)
    def _():
        for r in range(SPEC):
            @pl.when(lon != owner(r))
            def _():
                to_lon(a_ref.at[natural(r)], rowb.at[r // nl, lon], rows.at[0], rows.at[1 + r // nl], owner(r)).start()

    peers(lambda p: to_lon(seaw_ref.at[p], seab.at[pl.ds(rp * lon, rp)], seas.at[0], seas.at[1], p).start())
    lat_sends(coef_ref, coefr, csem)
    lat_sends(a_ref, halo, asem)

    @pl.when(polar)
    def _():
        for r in range(SPEC):
            @pl.when(lon == owner(r))
            def _():
                rowb[r // nl, lon] = a_ref[natural(r)]

    def own_sea(i, carry):
        seab[rp * lon + i] = seaw_ref[lon, i]
        return carry
    lax.fori_loop(0, rp, own_sea, 0)

    def clear(f, carry):
        z = jnp.zeros((8, LEV), f32)
        fa[f, pl.ds(0, 8), :] = z
        fa[f, pl.ds(WIDE - 16, 8), :] = z
        fa[f, pl.ds(WIDE - 8, 8), :] = z
        fb[f, pl.ds(0, 8), :] = z
        fb[f, pl.ds(WIDE - 8, 8), :] = z
        return carry
    lax.fori_loop(0, FRAMES, clear, 0)
    for f in (0, 1, 46, 47):
        fa[f] = jnp.zeros((WIDE, LEV), f32)
        fb[f] = jnp.zeros((WIDE, LEV), f32)
    fa[48] = jnp.zeros((WIDE, LEV), f32)
    fb[48] = jnp.zeros((WIDE, LEV), f32)

    def fill(m, carry):
        fa[m + 8, pl.ds(16, COLS), :] = a_ref[natural(m)]
        return carry
    lax.fori_loop(0, ROWS, fill, 0)

    col0 = jnp.broadcast_to(vmix_ref[:, 0:1], (LEV, LEV))
    rowid = lax.broadcasted_iota(jnp.int32, (LEV, LEV), 0)
    both = jnp.concatenate([vmix_ref[...], col0 + jnp.where(rowid == 0, 1.0, 0.0)], 1)
    bhi, blo = split(both)
    vb[0, pl.ds(0, LEV), :] = bhi
    vb[0, pl.ds(LEV, LEV), :] = bhi
    vb[1, pl.ds(0, LEV), :] = blo
    vb[1, pl.ds(LEV, LEV), :] = jnp.zeros_like(blo)

    def levels(x):
        both = jnp.concatenate(split(x), 1)
        res = dot(both, vb[0]) + dot(both, vb[1])
        return x + res[:, :LEV], res[:, LEV:]

    cour = cour_ref[...]
    east = 0.1 - 0.5 * cour
    west = 0.1 + 0.5 * cour
    lane1 = lax.broadcasted_iota(jnp.int32, (1, LEV), 1)
    vrow0 = vmix_ref[0:1, :] + jnp.where(lane1 == 0, 1.0, 0.0)
    half0 = jnp.where(lane1 == 0, 0.5, 0.0)
    kown = lon * kq + lax.rem(lax.broadcasted_iota(jnp.int32, (ko, LEV), 0), kq)
    olane = lax.broadcasted_iota(jnp.int32, (ko, LEV), 1)
    krow = lax.broadcasted_iota(jnp.int32, (2 * KW, LEV), 0)
    klane = lax.broadcasted_iota(jnp.int32, (2 * KW, LEV), 1)

    def swap(x, rowid):
        return jnp.where(lax.rem(rowid, ko) < kq, pltpu.roll(x, x.shape[0] - kq, 0), pltpu.roll(x, kq, 0))

    def cutoff(r):
        return cut_ref[jnp.where(flip, 2 * NPOLE - 1 - r, r)]

    mine = pl.ds(pl.multiple_of(lon * ko, 8), ko)

    @pl.when(polar)
    def _():
        cuts = jnp.full((1, LEV), KW, jnp.int32)
        for r in range(NPOLE):
            cuts = jnp.where(lane1 == r + 8, cutoff(r), cuts)
        kid = krow // ko * kq + lax.rem(krow, kq)
        keept[...] = jnp.where(kid <= cuts, 1.0, 0.0)
        for buf in (sa, sb):
            buf[0] = jnp.zeros((ko, LEV), f32)
            buf[SPEC + 1] = jnp.zeros((ko, LEV), f32)

    lat_recvs(halo, asem)
    for i in range(HALO):
        fa[40 + i, pl.ds(16, COLS), :] = halo[1, i]

    @pl.when(jnp.logical_not(polar))
    def _():
        for i in range(HALO):
            fa[2 + i, pl.ds(16, COLS), :] = halo[0, i]

    @pl.when(polar)
    def _():
        for i in range(HALO):
            fa[2 + i] = jnp.zeros((WIDE, LEV), f32)
            fb[2 + i] = jnp.zeros((WIDE, LEV), f32)

    def gather_rows(own_of, got):
        mt[...] = jnp.zeros_like(mt)

        def put(m, carry):
            mt[pl.ds(m + 8, 1), :] = own_of(m)
            return carry
        lax.fori_loop(0, ROWS, put, 0)
        for i in range(HALO):
            mt[40 + i:41 + i, :] = got[1, i]

        @pl.when(jnp.logical_not(polar))
        def _():
            for i in range(HALO):
                mt[2 + i:3 + i, :] = got[0, i]
        return mt[...].T

    lat_recvs(coefr, csem)
    fa[48, pl.ds(16, COLS), :] = gather_rows(lambda m: coef_ref[natural(m)], coefr)[:COLS]

    def pack(f, carry):
        sendx[0, f] = fa[f, pl.ds(16 + COLS - 8, 8), :]
        sendx[1, f] = fa[f, pl.ds(16, 8), :]
        return carry
    lax.fori_loop(2, FRAMES, pack, 0)
    zero = jnp.zeros((8, LEV), f32)
    for s in range(2):
        for f in range(2):
            sendx[s, f] = zero
    ahead = lax.rem(lon + 1, nl)
    behind = lax.rem(lon + nl - 1, nl)
    to_east = to_lon(sendx.at[0], recvx.at[0], xsem.at[0], xsem.at[2], ahead)
    to_west = to_lon(sendx.at[1], recvx.at[1], xsem.at[1], xsem.at[3], behind)
    to_east.start()
    to_west.start()

    wait_bytes(seab.at[pl.ds(0, ROWS - rp)], seas.at[1])
    lat_sends(seab, sear, searow)

    def across(u, x):
        return lax.dot_general(u, x, (((1,), (1,)), ((), ())), preferred_element_type=f32)

    @pl.when(polar)
    def _():
        loads[0].wait()
        loads[1].wait()
        ident = jnp.where(rowid == lax.broadcasted_iota(jnp.int32, (LEV, LEV), 1), 1.0, 0.0)
        ucol = split((vmix_ref[...] + ident).T[0:8, :])
        for slot in range(-(-SPEC // nl)):
            r = slot * nl + turn

            @pl.when(r < SPEC)
            def _():
                wait_bytes(rowb.at[slot, pl.ds(0, nl - 1)], rows.at[1 + slot])
                acc = jnp.zeros((2 * KW, LEV), f32)
                for g in range(GROUPS):
                    cols = rowb[slot, :, pl.ds(STARTS[g], GW), :].reshape(nl * GW, LEV)
                    tab = (ct[0, pl.ds(2 * KW * g, 2 * KW), :], ct[1, pl.ds(2 * KW * g, 2 * KW), :])
                    acc = acc + dot3n(tab, split(cols))
                spec[slot] = acc
                waved = wave_ref[0] * acc + wave_ref[1] * cour * swap(acc, krow)
                pair = split(jnp.concatenate([waved, acc], 0))
                low = across(ucol[0], pair[0]) + across(ucol[1], pair[0]) + across(ucol[0], pair[1])
                for i in range(4):
                    xs[slot, i:i + 1, :] = low[0:1, i * LEV:(i + 1) * LEV]
                    xr[r, i:i + 1, :] = low[0:1, i * LEV:(i + 1) * LEV]
                peers(lambda p: to_lon(xs.at[slot], xr.at[r], xss.at[0], xss.at[1], p).start())

                def chunk(p):
                    return spec.at[slot, pl.ds(pl.multiple_of(p * ko, 8), ko)]
                peers(lambda p: to_lon(chunk(p), sa.at[r + 1], kss.at[0], kss.at[1], p).start())
                sa[r + 1] = spec[slot, mine, :]

    lat_recvs(sear, searow)
    st0[...] = jnp.zeros_like(st0)
    st1[...] = jnp.zeros_like(st1)
    st0[pl.ds(Q0, QN), :] = gather_rows(lambda m: seab[natural(m)], sear)[:QN]

    to_east.wait_recv()
    to_west.wait_recv()

    def unpack(f, carry):
        fa[f, pl.ds(8, 8), :] = recvx[0, f]
        fa[f, pl.ds(16 + COLS, 8), :] = recvx[1, f]
        return carry
    lax.fori_loop(2, FRAMES, unpack, 0)
    coeft[...] = fa[48, pl.ds(Q0, QN), :]

    def evolve(t, src, dst):
        wc = wave_ref[0, mine, :]
        ws = wave_ref[1, mine, :] * cour
        adv = []
        for r in range(SPEC - 1 - t):
            here = src[r + 1]
            x = wc * here + ws * swap(here, lax.broadcasted_iota(jnp.int32, (ko, LEV), 0)) + 0.1 * (src[r] + src[r + 2])
            adv.append(jnp.where(kown <= cutoff(r), x, 0.0) if r < NPOLE else x)
        new, low = levels(jnp.concatenate(adv, 0))
        level0 = jnp.zeros((ko, LEV), f32)
        for r in range(SPEC - 1 - t):
            dst[r + 1] = new[r * ko:(r + 1) * ko]
            if r < NPOLE:
                level0 = jnp.where(olane == r + 8, low[r * ko:(r + 1) * ko], level0)
        ep[t, pl.ds(0, ko), :] = level0
        ep[t, pl.ds(ko, ko), :] = new[(NPOLE - 1) * ko:NPOLE * ko]

    def message(got, made, sems, t):
        got[t, lon] = made[t]
        peers(lambda p: to_lon(made.at[t], got.at[t, lon], sems.at[t, 0], sems.at[t, 1], p).start())

    def message_wait(got, sems, t, which):
        wait_bytes(got.at[t, pl.ds(0, nl - 1)], sems.at[t, which])

    extra = turn < SPEC % nl

    def others_rows(ref, sem):
        @pl.when(extra)
        def _():
            wait_bytes(ref.at[pl.ds(0, SPEC - SPEC // nl - 1)], sem)

        @pl.when(jnp.logical_not(extra))
        def _():
            wait_bytes(ref.at[pl.ds(0, SPEC - SPEC // nl)], sem)

    def first_level0():
        others_rows(xr, xss.at[1])
        mt[...] = jnp.zeros_like(mt)
        cols = []
        for i in range(4):
            for r in range(NPOLE + 1):
                mt[r + 8:r + 9, :] = xr[r, i:i + 1, :]
            cols.append(mt[...].T)
        own, beside = jnp.concatenate(cols[:2], 0), jnp.concatenate(cols[2:], 0)
        near = pltpu.roll(beside, 1, 1) + pltpu.roll(beside, LEV - 1, 1)
        return (own + 0.1 * near) * keept[...]

    def last_rows():
        loads[2].wait()
        for slot in range(-(-NPOLE // nl)):
            r = slot * nl + turn

            @pl.when(r < NPOLE)
            def _():
                wait_bytes(rs6.at[slot, pl.ds(0, nl - 1)], r6.at[1 + slot])
                waves = split(rs6[slot].reshape(2 * KW, LEV))
                fin[r] = dot3n((inva[0, lon], inva[1, lon]), waves)

                def one(p):
                    stage[slot, p] = dot3n((inva[0, p], inva[1, p]), waves)
                    to_lon(stage.at[slot, p], fin.at[r], fsem.at[0], fsem.at[1], p).start()
                peers(one)

    lane_ok = jnp.logical_or(lane >= 8, jnp.logical_not(polar))
    glane = lax.broadcasted_iota(jnp.int32, (GW, LEV), 1) // 21

    for t in range(1, STEPS + 1):
        src, dst = (fa, fb) if t % 2 else (fb, fa)
        sprev, snow = (sa, sb) if t % 2 else (sb, sa)
        sea, sea_next = (st0, st1) if t % 2 else (st1, st0)
        first = jnp.where(polar, 8 + NPOLE, 2 + t)
        count = jnp.where(polar, -(-(22 - t) // 4), -(-(44 - 2 * t) // 4))

        def grid_rows(i, acc):
            adv = []
            for j in range(4):
                f = first + 4 * i + j
                mid = pl.ds(Q0, QN)
                adv.append(0.6 * src[f, mid, :] + 0.1 * (src[f - 1, mid, :] + src[f + 1, mid, :])
                           + east * src[f, pl.ds(Q0 + 1, QN), :] + west * src[f, pl.ds(Q0 - 1, QN), :])
            new, low = levels(jnp.concatenate(adv, 0))
            for j in range(4):
                f = first + 4 * i + j
                dst[f, pl.ds(Q0, QN), :] = new[j * QN:(j + 1) * QN]
                acc = jnp.where(lane == f, low[j * QN:(j + 1) * QN], acc)
            return acc
        a0t[...] = lax.fori_loop(0, count, grid_rows, jnp.zeros((QN, LEV), f32))

        @pl.when(polar)
        def _():
            if t == STEPS:
                last_rows()
            if t > 1:
                message_wait(fx, fxs, t - 1, 1)
                got = split(fx[t - 1].reshape(nl * GW, LEV))
                res = jnp.zeros((2 * KW, LEV), f32)
                for g in range(GROUPS):
                    tab = (ct[0, pl.ds(2 * KW * g, 2 * KW), :], ct[1, pl.ds(2 * KW * g, 2 * KW), :])
                    res = jnp.where(klane // 21 == g, dot3n(tab, got), res)
                hats = dot(jnp.concatenate(split(res), 1), fold_ref[...])
                hat, near = hats[:, :LEV], hats[:, LEV:]
                add = wave_ref[0] * hat + wave_ref[1] * cour[:, 0:1] * swap(hat, krow) + 0.1 * near
                add = add * keept[...]
                at[...] = add
            if t == 1:
                res = dot3n((inv[0], inv[1]), split(first_level0()))
            else:
                message_wait(ex, exs, t - 1, 1)
                level0 = ex[t - 1, :, pl.ds(0, ko), :].reshape(2 * KW, LEV) + vrow0[:, 0:1] * add
                edge = ex[t - 1, :, pl.ds(ko, ko), :].reshape(2 * KW, LEV)
                edge = edge + add[:, 7 + NPOLE:8 + NPOLE] * vrow0 if t < STEPS else add
                res = dot3((inv[0], inv[1]), split(jnp.concatenate([level0, edge], 1)))
            filtered = jnp.logical_and(lane >= 8, lane < 8 + NPOLE)
            a0t[...] = jnp.where(filtered, res[:, :LEV], a0t[...])
            if t == STEPS:
                at[pl.ds(0, QN), :] = res[:, LEV:]
            elif t > 1:
                dst[7 + NPOLE, pl.ds(Q0, QN), :] = res[:, LEV:]

        now = sea[pl.ds(Q0, QN), :]
        flux = coeft[...] * (now - a0t[...])
        fluxt[...] = flux

        if t < STEPS:
            @pl.when(polar)
            def _():
                msg = jnp.zeros((GW, LEV), f32)
                for g in range(GROUPS):
                    turned = pltpu.roll(fluxt[pl.ds(8 + STARTS[g], GW), :], (21 * g - 8) % LEV, 1)
                    msg = jnp.where(glane == g, turned, msg)
                fp[t] = msg
                message(fx, fp, fxs, t)
                if t == 1:
                    others_rows(sa, kss.at[1])
                    evolve(0, sa, sb)
                    message(ex, ep, exs, 0)
                else:
                    own = at[mine, :]
                    for r in range(SPEC - t):
                        snow[r + 1] = snow[r + 1] + own[:, r + 8:r + 9] * vrow0
                evolve(t, snow, sprev)
                message(ex, ep, exs, t)
                if t == STEPS - 1:
                    for r in range(NPOLE):
                        @pl.when(lon != owner(r))
                        def _():
                            to_lon(sprev.at[r + 1], rs6.at[r // nl, lon], r6.at[0], r6.at[1 + r // nl], owner(r)).start()

                        @pl.when(lon == owner(r))
                        def _():
                            rs6[r // nl, lon] = sprev[r + 1]

        around = (pltpu.roll(now, 1, 1) + pltpu.roll(now, LEV - 1, 1)
                  + sea[pl.ds(Q0 - 1, QN), :] + sea[pl.ds(Q0 + 1, QN), :])
        later = now - 0.3 * flux + 0.2 * (around - 4.0 * now)
        sea_next[pl.ds(Q0, QN), :] = jnp.where(lane_ok, later, 0.0)

        if t == 1:
            @pl.when(polar)
            def _():
                message_wait(ex, exs, 0, 1)
                edge = ex[0, :, pl.ds(ko, ko), :].reshape(2 * KW, LEV)
                dst[7 + NPOLE, pl.ds(Q0, QN), :] = dot3n((inv[0], inv[1]), split(edge))

        def warm(f):
            dst[f, pl.ds(Q0, QN), :] = dst[f, pl.ds(Q0, QN), :] + flux[:, f:f + 1] * half0

        @pl.when(jnp.logical_not(polar))
        def _():
            for f in range(2 + t, 7 + NPOLE):
                warm(f)
        for f in range(7 + NPOLE, 46 - t):
            warm(f)

    last, sea = fa, st0

    mt[...] = sea[pl.ds(16, LEV), :].T

    def put_row(n, carry):
        seaf[n] = mt[pl.ds(natural(n) + 8, 1), :]
        return carry
    lax.fori_loop(0, ROWS, put_row, 0)
    peers(lambda p: to_lon(seaf.at[pl.ds(rp * p, rp)], seafin.at[lon], fins.at[0], fins.at[1], p).start())

    def own_fin(i, carry):
        seafin[lon, i] = seaf[rp * lon + i]
        return carry
    lax.fori_loop(0, rp, own_fin, 0)

    def give_grid(m, carry):
        out_ref[natural(m)] = last[m + 8, pl.ds(16, COLS), :]
        return carry
    lax.fori_loop(jnp.where(polar, NPOLE, 0), ROWS, give_grid, 0)

    @pl.when(polar)
    def _():
        more = turn < NPOLE % nl

        @pl.when(more)
        def _():
            wait_bytes(fin.at[pl.ds(0, NPOLE - NPOLE // nl - 1)], fsem.at[1])

        @pl.when(jnp.logical_not(more))
        def _():
            wait_bytes(fin.at[pl.ds(0, NPOLE - NPOLE // nl)], fsem.at[1])
        for r in range(NPOLE):
            out_ref[natural(r)] = (fin[r] + at[pl.ds(8, COLS), r + 8:r + 9] * vrow0
                                   + fluxt[pl.ds(8, COLS), r + 8:r + 9] * half0)

    wait_bytes(seafin.at[pl.ds(0, nl - 1)], fins.at[1])
    seaout_ref[...] = seafin[...]

    wait_bytes(seafin.at[pl.ds(0, nl - 1)], fins.at[0])
    wait_bytes(seab.at[pl.ds(0, ROWS - rp)], seas.at[0])
    lat_sent(halo, asem)
    lat_sent(coefr, csem)
    lat_sent(sear, searow)
    to_east.wait_send()
    to_west.wait_send()

    @pl.when(polar)
    def _():
        for r in range(SPEC):
            @pl.when(lon != owner(r))
            def _():
                wait_bytes(a_ref.at[0], rows.at[0])
        for slot in range(-(-SPEC // nl)):
            @pl.when(slot * nl + turn < SPEC)
            def _():
                wait_bytes(spec.at[slot, pl.ds(0, (nl - 1) * ko)], kss.at[0])
                peers(lambda p: wait_bytes(xs.at[slot], xss.at[0]))
        for t in range(STEPS):
            message_wait(ex, exs, t, 0)
        for t in range(1, STEPS):
            message_wait(fx, fxs, t, 0)
        for r in range(NPOLE):
            @pl.when(lon != owner(r))
            def _():
                wait_bytes(sa.at[0], r6.at[0])
        for slot in range(-(-NPOLE // nl)):
            @pl.when(slot * nl + turn < NPOLE)
            def _():
                wait_bytes(stage.at[slot, pl.ds(0, nl - 1)], fsem.at[0])


def local(nl, consts, air, sea, land, courant, vmix, cutoffs):
    rp = ROWS // nl
    ko = 2 * KW // nl
    blocks = sea.reshape(rp, nl, COLS)
    wide = jnp.concatenate([jnp.roll(blocks, 1, 1)[:, :, COLS - 8:], blocks, jnp.roll(blocks, -1, 1)[:, :, :8]], 2)
    wide = jnp.pad(wide, ((0, 0), (0, 0), (0, LEV - COLS - 16)))
    seaw = wide.transpose(1, 0, 2)[:, :, None, :]
    coef = jnp.pad(jnp.where(land == 1, 0.5, 0.15).astype(f32), ((0, 0), (0, LEV - COLS)))[:, None, :]
    inv, inva, ct, fold, wave = consts
    last = -(-NPOLE // nl)
    slots = -(-SPEC // nl)
    vm = pl.BlockSpec(memory_space=pltpu.VMEM)
    hbm = pl.BlockSpec(memory_space=pl.ANY)
    dma = pltpu.SemaphoreType.DMA
    v = pltpu.VMEM
    air_out, sea_out = pl.pallas_call(
        functools.partial(kernel, nl),
        out_shape=(jax.ShapeDtypeStruct((ROWS, COLS, LEV), f32),
                   jax.ShapeDtypeStruct((nl, rp, 1, LEV), f32)),
        in_specs=[vm, vm, vm, vm, vm, pl.BlockSpec(memory_space=pltpu.SMEM), hbm, hbm, hbm, vm, vm],
        out_specs=(vm, vm),
        scratch_shapes=[
            v((FRAMES, WIDE, LEV), f32), v((FRAMES, WIDE, LEV), f32),
            v((SPEC + 2, ko, LEV), f32), v((SPEC + 2, ko, LEV), f32),
            v((slots, nl, COLS, LEV), f32), v((slots, 2 * KW, LEV), f32),
            v((STEPS, nl, GW, LEV), f32), v((STEPS, GW, LEV), f32),
            v((STEPS, nl, 2 * ko, LEV), f32), v((STEPS, 2 * ko, LEV), f32),
            v((last, nl, ko, LEV), f32), v((last, nl, COLS, LEV), f32), v((NPOLE, COLS, LEV), f32),
            v((slots, 4, LEV), f32), v((SPEC, 4, LEV), f32),
            v((2, HALO, COLS, LEV), f32), v((2, HALO, 1, LEV), f32), v((2, HALO, 1, LEV), f32),
            v((ROWS, 1, LEV), f32), v((ROWS, 1, LEV), f32), v((nl, rp, 1, LEV), f32),
            v((2, FRAMES, 8, LEV), f32), v((2, FRAMES, 8, LEV), f32),
            v((2, QN, 2 * KW), bf16), v((2, nl, COLS, 2 * KW), bf16), v((2, GROUPS * 2 * KW, nl * GW), bf16),
            v((2, 2 * LEV, 2 * LEV), bf16), v((LEV, LEV), f32),
            v((QN, LEV), f32), v((QN, LEV), f32), v((144, LEV), f32), v((144, LEV), f32),
            v((QN, LEV), f32), v((2 * KW, LEV), f32), v((2 * KW, LEV), f32),
            dma((3,)), dma((4,)), dma((4,)), dma((2,)), dma((4,)), dma((4,)), dma((1 + slots,)), dma((2,)),
            dma((STEPS, 2)), dma((STEPS, 2)), dma((1 + last,)), dma((2,)), dma((2,)), dma((2,)),
        ],
        compiler_params=pltpu.CompilerParams(
            collective_id=0, has_side_effects=True, vmem_limit_bytes=56 * 1024 * 1024),
    )(air, seaw, coef, courant.reshape(1, LEV), vmix, cutoffs, inv, inva, ct, fold, wave)
    sea_out = sea_out[:, :, 0, :COLS].transpose(1, 0, 2).reshape(rp, nl * COLS)
    return air_out, sea_out


def solution(mesh):
    nl = mesh.shape["lon"]
    consts = tuple(jnp.asarray(x) for x in tables(nl))
    placed = (P("lat", "lon", None), P(("lat", "lon"), None), P("lat", "lon"), P(), P(), P())

    def run(*args):
        return jax.shard_map(
            functools.partial(local, nl),
            mesh=mesh,
            in_specs=((P(),) * 5,) + placed,
            out_specs=(P("lat", "lon", None), P(("lat", "lon"), None)),
            check_vma=False,
        )(consts, *args)

    return run
```

```python
import functools

import jax
import jax.numpy as jnp
import ml_dtypes
import numpy as np
from jax import lax
from jax.experimental import pallas as pl
from jax.experimental.pallas import tpu as pltpu
from jax.sharding import PartitionSpec as P

STEPS = 6
NPOLE = 16
ROWS = 32
COLS = 90
KW = 128
LEV = 128
HALO = 6
FRAMES = 49
WIDE = 120
Q0, QN = 8, 104
SPEC = NPOLE + HALO
GROUPS, GW = 6, 16
STARTS = (0, 15, 30, 45, 60, 74)

f32, bf16 = jnp.float32, jnp.bfloat16
MESH = pl.DeviceIdType.MESH


def split(x):
    hi = x.astype(bf16)
    return hi, (x - hi.astype(f32)).astype(bf16)


def dot(a, b):
    return jnp.dot(a, b, preferred_element_type=f32)


def dot3(a, b):
    return dot(a[0], b[0]) + dot(a[1], b[0]) + dot(a[0], b[1])


def dot3n(a, b):
    n = b[0].shape[1]
    both = dot(a[0], jnp.concatenate(b, 1))
    return both[:, :n] + both[:, n:] + dot(a[1], b[0])


def np_split(x):
    x = x.astype(np.float32)
    hi = x.astype(ml_dtypes.bfloat16)
    lo = (x - hi.astype(np.float32)).astype(ml_dtypes.bfloat16)
    return np.stack([hi, lo])


def tables(nl):
    nlon = nl * COLS
    kq = KW // nl
    k = (np.arange(nl)[:, None, None] * kq + np.arange(kq)[None, None, :]) * np.ones((1, 2, 1), int)
    sine = np.broadcast_to(np.arange(2)[None, :, None], k.shape).reshape(-1)
    k = k.reshape(-1)

    def fwd(c):
        ang = (c[..., None] * k % nlon) * (2.0 * np.pi / nlon)
        return np.where(sine == 0, np.cos(ang), np.sin(ang))

    d = np.arange(nl)[:, None]
    q = np.arange(QN)[None]
    weight = np.where(k == 0, 1.0, 2.0) / nlon
    inv = np.moveaxis(np_split(fwd((d * COLS + q - 8) % nlon) * weight), 0, 1)
    everywhere = np_split(fwd(np.arange(nl * COLS).reshape(nl, COLS)) * weight)
    packed = []
    for g in range(GROUPS):
        c = STARTS[g] + np.arange(GW)[None]
        ours = np.logical_and(c >= g * 15, c < g * 15 + 15)
        packed.append(np.where(ours[..., None], fwd(d * COLS + c), 0.0).reshape(nl * GW, 2 * KW).T)
    fold = np.zeros((LEV, 2 * LEV))
    for g in range(GROUPS):
        for r in range(SPEC - 1):
            fold[21 * g + r, r + 8] = 0.5
            for near in (r - 1, r + 1):
                if near >= 0:
                    fold[21 * g + r, LEV + near + 8] = 0.5
    fold = np.concatenate([fold, fold]).astype(ml_dtypes.bfloat16)
    step = 2.0 * np.pi / nlon
    wave = np.stack([0.6 + 0.2 * np.cos(k * step), np.where(sine == 0, -1.0, 1.0) * np.sin(k * step)])
    wave = np.broadcast_to(wave[:, :, None], (2, 2 * KW, LEV)).astype(np.float32)
    return inv, everywhere, np_split(np.concatenate(packed, 0)), fold, wave


def kernel(nl, a_hbm, seaw_ref, land_ref, cour_ref, vmix_ref, cut_ref, inv_hbm, all_hbm, ct_hbm, fold_ref,
           wave_ref, out_hbm, seaout_ref, a_ref, out_ref, coef_ref, fa, fb, sa, sb, rowb, spec, fx, fp, ex, ep, rs6, stage, fin, xs, xr, halo, coefr, sear,
           seab, seaf, seafin, sendx, recvx, inv, inva, ct, vb, mt, a0t, coeft, st0, st1, fluxt,
           at, keept, tsem, asem, csem, seas, searow, xsem, rows, kss, fxs, exs, r6, fsem, xss, fins, isem, osem):
    lat, lon = lax.axis_index("lat"), lax.axis_index("lon")
    polar = jnp.logical_or(lat == 0, lat == 3)
    flip = lat == 3
    kq = KW // nl
    ko = 2 * kq
    rp = ROWS // nl
    half = nl // 2
    turn = lax.rem(lon, half) * 2 + lon // half
    lane = lax.broadcasted_iota(jnp.int32, (QN, LEV), 1)

    def natural(m):
        return jnp.where(flip, ROWS - 1 - m, m)

    def peers(body):
        def one(i, carry):
            body(lax.rem(lon + i, nl))
            return carry
        lax.fori_loop(1, nl, one, 0)

    def wait_bytes(ref, sem):
        pltpu.make_async_copy(ref, ref, sem).wait()

    def to_lon(src, dst, ssem, rsem, peer):
        return pltpu.make_async_remote_copy(src, dst, ssem, rsem, device_id={"lon": peer},
                                            device_id_type=MESH)

    loads = [
        pltpu.make_async_copy(inv_hbm.at[lon], inv, tsem.at[0]),
        pltpu.make_async_copy(ct_hbm, ct, tsem.at[1]),
        pltpu.make_async_copy(all_hbm, inva, tsem.at[2]),
    ]

    @pl.when(polar)
    def _():
        for load in loads:
            load.start()

    rows_in = [pltpu.make_async_copy(a_hbm.at[:, m, :], a_ref.at[m], isem) for m in range(ROWS)]
    for row in rows_in:
        row.start()

    barrier = pltpu.get_barrier_semaphore()
    peers(lambda p: pl.semaphore_signal(barrier, inc=1, device_id={"lon": p}, device_id_type=MESH))

    @pl.when(lat < 3)
    def _():
        pl.semaphore_signal(barrier, inc=1, device_id={"lat": lat + 1}, device_id_type=MESH)

    @pl.when(lat > 0)
    def _():
        pl.semaphore_signal(barrier, inc=1, device_id={"lat": lat - 1}, device_id_type=MESH)

    pl.semaphore_wait(barrier, nl - 1 + jnp.where(polar, 1, 2))

    def own_coef(m, carry):
        coef_ref[m] = jnp.zeros((1, LEV), f32)
        coef_ref[m, :, pl.ds(0, COLS)] = jnp.where(land_ref[pl.ds(m, 1), :] == 1, 0.5, 0.15)
        return carry
    lax.fori_loop(0, ROWS, own_coef, 0)
    wait_bytes(a_ref, isem)

    side = jnp.where(lat == 2, 1, 0)

    def lat_sends(src_ref, dst_ref, sems):
        def make(src, s, i, which, to):
            return pltpu.make_async_remote_copy(
                src_ref.at[src], dst_ref.at[s, i], sems.at[which], sems.at[2 + s],
                device_id={"lat": to}, device_id_type=MESH)

        @pl.when(lat < 3)
        def _():
            for i in range(HALO):
                make(jnp.where(lat == 2, ROWS - 1 - i, ROWS - HALO + i), side, i, 0, lat + 1).start()

        @pl.when(lat > 0)
        def _():
            for i in range(HALO):
                make(i, 1, i, 1, lat - 1).start()

    def lat_recvs(dst_ref, sems):
        wait_bytes(dst_ref.at[1], sems.at[3])

        @pl.when(jnp.logical_not(polar))
        def _():
            wait_bytes(dst_ref.at[0], sems.at[2])

    def lat_sent(dst_ref, sems):
        @pl.when(lat < 3)
        def _():
            wait_bytes(dst_ref.at[0], sems.at[0])

        @pl.when(lat > 0)
        def _():
            wait_bytes(dst_ref.at[0], sems.at[1])

    def owner(r):
        return (r % nl) % 2 * half + r % nl // 2

    @pl.when(polar)
    def _():
        for r in range(SPEC):
            @pl.when(lon != owner(r))
            def _():
                to_lon(a_ref.at[natural(r)], rowb.at[r // nl, lon], rows.at[0], rows.at[1 + r // nl], owner(r)).start()

    peers(lambda p: to_lon(seaw_ref.at[p], seab.at[pl.ds(rp * lon, rp)], seas.at[0], seas.at[1], p).start())
    lat_sends(coef_ref, coefr, csem)
    lat_sends(a_ref, halo, asem)

    @pl.when(polar)
    def _():
        for r in range(SPEC):
            @pl.when(lon == owner(r))
            def _():
                rowb[r // nl, lon] = a_ref[natural(r)]

    def own_sea(i, carry):
        seab[rp * lon + i] = seaw_ref[lon, i]
        return carry
    lax.fori_loop(0, rp, own_sea, 0)

    def clear(f, carry):
        z = jnp.zeros((8, LEV), f32)
        fa[f, pl.ds(0, 8), :] = z
        fa[f, pl.ds(WIDE - 16, 8), :] = z
        fa[f, pl.ds(WIDE - 8, 8), :] = z
        fb[f, pl.ds(0, 8), :] = z
        fb[f, pl.ds(WIDE - 8, 8), :] = z
        return carry
    lax.fori_loop(0, FRAMES, clear, 0)
    for f in (0, 1, 46, 47):
        fa[f] = jnp.zeros((WIDE, LEV), f32)
        fb[f] = jnp.zeros((WIDE, LEV), f32)
    fa[48] = jnp.zeros((WIDE, LEV), f32)
    fb[48] = jnp.zeros((WIDE, LEV), f32)

    def fill(m, carry):
        fa[m + 8, pl.ds(16, COLS), :] = a_ref[natural(m)]
        return carry
    lax.fori_loop(0, ROWS, fill, 0)

    col0 = jnp.broadcast_to(vmix_ref[:, 0:1], (LEV, LEV))
    rowid = lax.broadcasted_iota(jnp.int32, (LEV, LEV), 0)
    both = jnp.concatenate([vmix_ref[...], col0 + jnp.where(rowid == 0, 1.0, 0.0)], 1)
    bhi, blo = split(both)
    vb[0, pl.ds(0, LEV), :] = bhi
    vb[0, pl.ds(LEV, LEV), :] = bhi
    vb[1, pl.ds(0, LEV), :] = blo
    vb[1, pl.ds(LEV, LEV), :] = jnp.zeros_like(blo)

    def levels(x):
        both = jnp.concatenate(split(x), 1)
        res = dot(both, vb[0]) + dot(both, vb[1])
        return x + res[:, :LEV], res[:, LEV:]

    cour = cour_ref[...]
    east = 0.1 - 0.5 * cour
    west = 0.1 + 0.5 * cour
    lane1 = lax.broadcasted_iota(jnp.int32, (1, LEV), 1)
    vrow0 = vmix_ref[0:1, :] + jnp.where(lane1 == 0, 1.0, 0.0)
    half0 = jnp.where(lane1 == 0, 0.5, 0.0)
    kown = lon * kq + lax.rem(lax.broadcasted_iota(jnp.int32, (ko, LEV), 0), kq)
    olane = lax.broadcasted_iota(jnp.int32, (ko, LEV), 1)
    krow = lax.broadcasted_iota(jnp.int32, (2 * KW, LEV), 0)
    klane = lax.broadcasted_iota(jnp.int32, (2 * KW, LEV), 1)

    def swap(x, rowid):
        return jnp.where(lax.rem(rowid, ko) < kq, pltpu.roll(x, x.shape[0] - kq, 0), pltpu.roll(x, kq, 0))

    def cutoff(r):
        return cut_ref[jnp.where(flip, 2 * NPOLE - 1 - r, r)]

    mine = pl.ds(pl.multiple_of(lon * ko, 8), ko)

    @pl.when(polar)
    def _():
        cuts = jnp.full((1, LEV), KW, jnp.int32)
        for r in range(NPOLE):
            cuts = jnp.where(lane1 == r + 8, cutoff(r), cuts)
        kid = krow // ko * kq + lax.rem(krow, kq)
        keept[...] = jnp.where(kid <= cuts, 1.0, 0.0)
        for buf in (sa, sb):
            buf[0] = jnp.zeros((ko, LEV), f32)
            buf[SPEC + 1] = jnp.zeros((ko, LEV), f32)

    lat_recvs(halo, asem)
    for i in range(HALO):
        fa[40 + i, pl.ds(16, COLS), :] = halo[1, i]

    @pl.when(jnp.logical_not(polar))
    def _():
        for i in range(HALO):
            fa[2 + i, pl.ds(16, COLS), :] = halo[0, i]

    @pl.when(polar)
    def _():
        for i in range(HALO):
            fa[2 + i] = jnp.zeros((WIDE, LEV), f32)
            fb[2 + i] = jnp.zeros((WIDE, LEV), f32)

    def gather_rows(own_of, got):
        mt[...] = jnp.zeros_like(mt)

        def put(m, carry):
            mt[pl.ds(m + 8, 1), :] = own_of(m)
            return carry
        lax.fori_loop(0, ROWS, put, 0)
        for i in range(HALO):
            mt[40 + i:41 + i, :] = got[1, i]

        @pl.when(jnp.logical_not(polar))
        def _():
            for i in range(HALO):
                mt[2 + i:3 + i, :] = got[0, i]
        return mt[...].T

    lat_recvs(coefr, csem)
    fa[48, pl.ds(16, COLS), :] = gather_rows(lambda m: coef_ref[natural(m)], coefr)[:COLS]

    def pack(f, carry):
        sendx[0, f] = fa[f, pl.ds(16 + COLS - 8, 8), :]
        sendx[1, f] = fa[f, pl.ds(16, 8), :]
        return carry
    lax.fori_loop(2, FRAMES, pack, 0)
    zero = jnp.zeros((8, LEV), f32)
    for s in range(2):
        for f in range(2):
            sendx[s, f] = zero
    ahead = lax.rem(lon + 1, nl)
    behind = lax.rem(lon + nl - 1, nl)
    to_east = to_lon(sendx.at[0], recvx.at[0], xsem.at[0], xsem.at[2], ahead)
    to_west = to_lon(sendx.at[1], recvx.at[1], xsem.at[1], xsem.at[3], behind)
    to_east.start()
    to_west.start()

    wait_bytes(seab.at[pl.ds(0, ROWS - rp)], seas.at[1])
    lat_sends(seab, sear, searow)

    def across(u, x):
        return lax.dot_general(u, x, (((1,), (1,)), ((), ())), preferred_element_type=f32)

    @pl.when(polar)
    def _():
        loads[0].wait()
        loads[1].wait()
        ident = jnp.where(rowid == lax.broadcasted_iota(jnp.int32, (LEV, LEV), 1), 1.0, 0.0)
        ucol = split((vmix_ref[...] + ident).T[0:8, :])
        for slot in range(-(-SPEC // nl)):
            r = slot * nl + turn

            @pl.when(r < SPEC)
            def _():
                wait_bytes(rowb.at[slot, pl.ds(0, nl - 1)], rows.at[1 + slot])
                acc = jnp.zeros((2 * KW, LEV), f32)
                for g in range(GROUPS):
                    cols = rowb[slot, :, pl.ds(STARTS[g], GW), :].reshape(nl * GW, LEV)
                    tab = (ct[0, pl.ds(2 * KW * g, 2 * KW), :], ct[1, pl.ds(2 * KW * g, 2 * KW), :])
                    acc = acc + dot3n(tab, split(cols))
                spec[slot] = acc
                waved = wave_ref[0] * acc + wave_ref[1] * cour * swap(acc, krow)
                pair = split(jnp.concatenate([waved, acc], 0))
                low = across(ucol[0], pair[0]) + across(ucol[1], pair[0]) + across(ucol[0], pair[1])
                for i in range(4):
                    xs[slot, i:i + 1, :] = low[0:1, i * LEV:(i + 1) * LEV]
                    xr[r, i:i + 1, :] = low[0:1, i * LEV:(i + 1) * LEV]
                peers(lambda p: to_lon(xs.at[slot], xr.at[r], xss.at[0], xss.at[1], p).start())

                def chunk(p):
                    return spec.at[slot, pl.ds(pl.multiple_of(p * ko, 8), ko)]
                peers(lambda p: to_lon(chunk(p), sa.at[r + 1], kss.at[0], kss.at[1], p).start())
                sa[r + 1] = spec[slot, mine, :]

    lat_recvs(sear, searow)
    st0[...] = jnp.zeros_like(st0)
    st1[...] = jnp.zeros_like(st1)
    st0[pl.ds(Q0, QN), :] = gather_rows(lambda m: seab[natural(m)], sear)[:QN]

    to_east.wait_recv()
    to_west.wait_recv()

    def unpack(f, carry):
        fa[f, pl.ds(8, 8), :] = recvx[0, f]
        fa[f, pl.ds(16 + COLS, 8), :] = recvx[1, f]
        return carry
    lax.fori_loop(2, FRAMES, unpack, 0)
    coeft[...] = fa[48, pl.ds(Q0, QN), :]

    def evolve(t, src, dst):
        wc = wave_ref[0, mine, :]
        ws = wave_ref[1, mine, :] * cour
        adv = []
        for r in range(SPEC - 1 - t):
            here = src[r + 1]
            x = wc * here + ws * swap(here, lax.broadcasted_iota(jnp.int32, (ko, LEV), 0)) + 0.1 * (src[r] + src[r + 2])
            adv.append(jnp.where(kown <= cutoff(r), x, 0.0) if r < NPOLE else x)
        new, low = levels(jnp.concatenate(adv, 0))
        level0 = jnp.zeros((ko, LEV), f32)
        for r in range(SPEC - 1 - t):
            dst[r + 1] = new[r * ko:(r + 1) * ko]
            if r < NPOLE:
                level0 = jnp.where(olane == r + 8, low[r * ko:(r + 1) * ko], level0)
        ep[t, pl.ds(0, ko), :] = level0
        ep[t, pl.ds(ko, ko), :] = new[(NPOLE - 1) * ko:NPOLE * ko]

    def message(got, made, sems, t):
        got[t, lon] = made[t]
        peers(lambda p: to_lon(made.at[t], got.at[t, lon], sems.at[t, 0], sems.at[t, 1], p).start())

    def message_wait(got, sems, t, which):
        wait_bytes(got.at[t, pl.ds(0, nl - 1)], sems.at[t, which])

    extra = turn < SPEC % nl

    def others_rows(ref, sem):
        @pl.when(extra)
        def _():
            wait_bytes(ref.at[pl.ds(0, SPEC - SPEC // nl - 1)], sem)

        @pl.when(jnp.logical_not(extra))
        def _():
            wait_bytes(ref.at[pl.ds(0, SPEC - SPEC // nl)], sem)

    def first_level0():
        others_rows(xr, xss.at[1])
        mt[...] = jnp.zeros_like(mt)
        cols = []
        for i in range(4):
            for r in range(NPOLE + 1):
                mt[r + 8:r + 9, :] = xr[r, i:i + 1, :]
            cols.append(mt[...].T)
        own, beside = jnp.concatenate(cols[:2], 0), jnp.concatenate(cols[2:], 0)
        near = pltpu.roll(beside, 1, 1) + pltpu.roll(beside, LEV - 1, 1)
        return (own + 0.1 * near) * keept[...]

    def last_rows():
        loads[2].wait()
        here = lax.rem(lon, half)
        base = lon - here
        for slot in range(NPOLE // half):
            r = slot * half + here
            wait_bytes(rs6.at[slot, pl.ds(0, nl - 1)], r6.at[1 + slot])
            waves = split(rs6[slot].reshape(2 * KW, LEV))

            def one(i, carry):
                at_i = lax.rem(here + i, half)
                p = base + at_i
                stage[slot, at_i] = dot3n((inva[0, p], inva[1, p]), waves)
                to_lon(stage.at[slot, at_i], fin.at[r], fsem.at[0], fsem.at[1], p).start()
                return carry
            lax.fori_loop(1, half, one, 0)
            fin[r] = dot3n((inva[0, lon], inva[1, lon]), waves)

    lane_ok = jnp.logical_or(lane >= 8, jnp.logical_not(polar))
    glane = lax.broadcasted_iota(jnp.int32, (GW, LEV), 1) // 21

    for t in range(1, STEPS + 1):
        src, dst = (fa, fb) if t % 2 else (fb, fa)
        sprev, snow = (sa, sb) if t % 2 else (sb, sa)
        sea, sea_next = (st0, st1) if t % 2 else (st1, st0)
        first = jnp.where(polar, 8 + NPOLE, 2 + t)
        count = jnp.where(polar, -(-(22 - t) // 4), -(-(44 - 2 * t) // 4))

        def grid_rows(i, acc):
            adv = []
            for j in range(4):
                f = first + 4 * i + j
                mid = pl.ds(Q0, QN)
                adv.append(0.6 * src[f, mid, :] + 0.1 * (src[f - 1, mid, :] + src[f + 1, mid, :])
                           + east * src[f, pl.ds(Q0 + 1, QN), :] + west * src[f, pl.ds(Q0 - 1, QN), :])
            new, low = levels(jnp.concatenate(adv, 0))
            for j in range(4):
                f = first + 4 * i + j
                dst[f, pl.ds(Q0, QN), :] = new[j * QN:(j + 1) * QN]
                acc = jnp.where(lane == f, low[j * QN:(j + 1) * QN], acc)
            return acc
        a0t[...] = lax.fori_loop(0, count, grid_rows, jnp.zeros((QN, LEV), f32))

        @pl.when(polar)
        def _():
            if t == STEPS:
                last_rows()
            if t > 1:
                message_wait(fx, fxs, t - 1, 1)
                got = split(fx[t - 1].reshape(nl * GW, LEV))
                res = jnp.zeros((2 * KW, LEV), f32)
                for g in range(GROUPS):
                    tab = (ct[0, pl.ds(2 * KW * g, 2 * KW), :], ct[1, pl.ds(2 * KW * g, 2 * KW), :])
                    res = jnp.where(klane // 21 == g, dot3n(tab, got), res)
                hats = dot(jnp.concatenate(split(res), 1), fold_ref[...])
                hat, near = hats[:, :LEV], hats[:, LEV:]
                add = wave_ref[0] * hat + wave_ref[1] * cour[:, 0:1] * swap(hat, krow) + 0.1 * near
                add = add * keept[...]
                at[...] = add
            if t == 1:
                res = dot3n((inv[0], inv[1]), split(first_level0()))
            else:
                message_wait(ex, exs, t - 1, 1)
                level0 = ex[t - 1, :, pl.ds(0, ko), :].reshape(2 * KW, LEV) + vrow0[:, 0:1] * add
                edge = ex[t - 1, :, pl.ds(ko, ko), :].reshape(2 * KW, LEV)
                edge = edge + add[:, 7 + NPOLE:8 + NPOLE] * vrow0 if t < STEPS else add
                res = dot3((inv[0], inv[1]), split(jnp.concatenate([level0, edge], 1)))
            filtered = jnp.logical_and(lane >= 8, lane < 8 + NPOLE)
            a0t[...] = jnp.where(filtered, res[:, :LEV], a0t[...])
            if t == STEPS:
                at[pl.ds(0, QN), :] = res[:, LEV:]
            elif t > 1:
                dst[7 + NPOLE, pl.ds(Q0, QN), :] = res[:, LEV:]

        now = sea[pl.ds(Q0, QN), :]
        flux = coeft[...] * (now - a0t[...])
        fluxt[...] = flux

        if t < STEPS:
            @pl.when(polar)
            def _():
                msg = jnp.zeros((GW, LEV), f32)
                for g in range(GROUPS):
                    turned = pltpu.roll(fluxt[pl.ds(8 + STARTS[g], GW), :], (21 * g - 8) % LEV, 1)
                    msg = jnp.where(glane == g, turned, msg)
                fp[t] = msg
                message(fx, fp, fxs, t)
                if t == 1:
                    others_rows(sa, kss.at[1])
                    evolve(0, sa, sb)
                    message(ex, ep, exs, 0)
                else:
                    own = at[mine, :]
                    for r in range(SPEC - t):
                        snow[r + 1] = snow[r + 1] + own[:, r + 8:r + 9] * vrow0
                evolve(t, snow, sprev)
                message(ex, ep, exs, t)
                if t == STEPS - 1:
                    for r in range(NPOLE):
                        for dev in (r % half, half + r % half):
                            @pl.when(lon != dev)
                            def _():
                                to_lon(sprev.at[r + 1], rs6.at[r // half, lon], r6.at[0], r6.at[1 + r // half], dev).start()

                            @pl.when(lon == dev)
                            def _():
                                rs6[r // half, lon] = sprev[r + 1]

        around = (pltpu.roll(now, 1, 1) + pltpu.roll(now, LEV - 1, 1)
                  + sea[pl.ds(Q0 - 1, QN), :] + sea[pl.ds(Q0 + 1, QN), :])
        later = now - 0.3 * flux + 0.2 * (around - 4.0 * now)
        sea_next[pl.ds(Q0, QN), :] = jnp.where(lane_ok, later, 0.0)

        if t == 1:
            @pl.when(polar)
            def _():
                message_wait(ex, exs, 0, 1)
                edge = ex[0, :, pl.ds(ko, ko), :].reshape(2 * KW, LEV)
                dst[7 + NPOLE, pl.ds(Q0, QN), :] = dot3n((inv[0], inv[1]), split(edge))

        def warm(f):
            dst[f, pl.ds(Q0, QN), :] = dst[f, pl.ds(Q0, QN), :] + fluxt[:, f:f + 1] * half0

        def warm_all():
            @pl.when(jnp.logical_not(polar))
            def _():
                for f in range(2 + t, 7 + NPOLE):
                    warm(f)
            for f in range(7 + NPOLE, 46 - t):
                warm(f)
        if t < STEPS:
            warm_all()

    last, sea = fa, st0

    mt[...] = sea[pl.ds(16, LEV), :].T

    def put_row(n, carry):
        seaf[n] = mt[pl.ds(natural(n) + 8, 1), :]
        return carry
    lax.fori_loop(0, ROWS, put_row, 0)
    peers(lambda p: to_lon(seaf.at[pl.ds(rp * p, rp)], seafin.at[lon], fins.at[0], fins.at[1], p).start())

    def own_fin(i, carry):
        seafin[lon, i] = seaf[rp * lon + i]
        return carry
    lax.fori_loop(0, rp, own_fin, 0)

    warm_all()

    def give_grid(m, carry):
        out_ref[natural(m)] = last[m + 8, pl.ds(16, COLS), :]
        return carry
    lax.fori_loop(jnp.where(polar, NPOLE, 0), ROWS, give_grid, 0)

    def row_out(m):
        n = natural(m)
        pltpu.make_async_copy(out_ref.at[n], out_hbm.at[:, n, :], osem).start()

    for m in range(NPOLE, ROWS):
        row_out(m)

    @pl.when(jnp.logical_not(polar))
    def _():
        for m in range(NPOLE):
            row_out(m)

    @pl.when(polar)
    def _():
        wait_bytes(fin.at[pl.ds(0, NPOLE - NPOLE // half)], fsem.at[1])
        for r in range(NPOLE):
            out_ref[natural(r)] = (fin[r] + at[pl.ds(8, COLS), r + 8:r + 9] * vrow0
                                   + fluxt[pl.ds(8, COLS), r + 8:r + 9] * half0)
            row_out(r)

    wait_bytes(seafin.at[pl.ds(0, nl - 1)], fins.at[1])
    seaout_ref[...] = seafin[...]

    wait_bytes(out_ref, osem)
    wait_bytes(seafin.at[pl.ds(0, nl - 1)], fins.at[0])
    wait_bytes(seab.at[pl.ds(0, ROWS - rp)], seas.at[0])
    lat_sent(halo, asem)
    lat_sent(coefr, csem)
    lat_sent(sear, searow)
    to_east.wait_send()
    to_west.wait_send()

    @pl.when(polar)
    def _():
        for r in range(SPEC):
            @pl.when(lon != owner(r))
            def _():
                wait_bytes(a_ref.at[0], rows.at[0])
        for slot in range(-(-SPEC // nl)):
            @pl.when(slot * nl + turn < SPEC)
            def _():
                wait_bytes(spec.at[slot, pl.ds(0, (nl - 1) * ko)], kss.at[0])
                peers(lambda p: wait_bytes(xs.at[slot], xss.at[0]))
        for t in range(STEPS):
            message_wait(ex, exs, t, 0)
        for t in range(1, STEPS):
            message_wait(fx, fxs, t, 0)
        for r in range(NPOLE):
            for dev in (r % half, half + r % half):
                @pl.when(lon != dev)
                def _():
                    wait_bytes(sa.at[0], r6.at[0])
        for slot in range(NPOLE // half):
            wait_bytes(stage.at[slot, pl.ds(0, half - 1)], fsem.at[0])


def local(nl, consts, air, sea, land, courant, vmix, cutoffs):
    rp = ROWS // nl
    ko = 2 * KW // nl
    blocks = sea.reshape(rp, nl, COLS)
    wide = jnp.concatenate([jnp.roll(blocks, 1, 1)[:, :, COLS - 8:], blocks, jnp.roll(blocks, -1, 1)[:, :, :8]], 2)
    wide = jnp.pad(wide, ((0, 0), (0, 0), (0, LEV - COLS - 16)))
    seaw = wide.transpose(1, 0, 2)[:, :, None, :]
    inv, inva, ct, fold, wave = consts
    half = nl // 2
    last = NPOLE // half
    slots = -(-SPEC // nl)
    vm = pl.BlockSpec(memory_space=pltpu.VMEM)
    hbm = pl.BlockSpec(memory_space=pl.ANY)
    dma = pltpu.SemaphoreType.DMA
    v = pltpu.VMEM
    air_out, sea_out = pl.pallas_call(
        functools.partial(kernel, nl),
        out_shape=(jax.ShapeDtypeStruct((COLS, ROWS, LEV), f32),
                   jax.ShapeDtypeStruct((nl, rp, 1, LEV), f32)),
        in_specs=[hbm, vm, vm, vm, vm, pl.BlockSpec(memory_space=pltpu.SMEM), hbm, hbm, hbm, vm, vm],
        out_specs=(hbm, vm),
        scratch_shapes=[
            v((ROWS, COLS, LEV), f32), v((ROWS, COLS, LEV), f32), v((ROWS, 1, LEV), f32),
            v((FRAMES, WIDE, LEV), f32), v((FRAMES, WIDE, LEV), f32),
            v((SPEC + 2, ko, LEV), f32), v((SPEC + 2, ko, LEV), f32),
            v((slots, nl, COLS, LEV), f32), v((slots, 2 * KW, LEV), f32),
            v((STEPS, nl, GW, LEV), f32), v((STEPS, GW, LEV), f32),
            v((STEPS, nl, 2 * ko, LEV), f32), v((STEPS, 2 * ko, LEV), f32),
            v((last, nl, ko, LEV), f32), v((last, half, COLS, LEV), f32), v((NPOLE, COLS, LEV), f32),
            v((slots, 4, LEV), f32), v((SPEC, 4, LEV), f32),
            v((2, HALO, COLS, LEV), f32), v((2, HALO, 1, LEV), f32), v((2, HALO, 1, LEV), f32),
            v((ROWS, 1, LEV), f32), v((ROWS, 1, LEV), f32), v((nl, rp, 1, LEV), f32),
            v((2, FRAMES, 8, LEV), f32), v((2, FRAMES, 8, LEV), f32),
            v((2, QN, 2 * KW), bf16), v((2, nl, COLS, 2 * KW), bf16), v((2, GROUPS * 2 * KW, nl * GW), bf16),
            v((2, 2 * LEV, 2 * LEV), bf16), v((LEV, LEV), f32),
            v((QN, LEV), f32), v((QN, LEV), f32), v((144, LEV), f32), v((144, LEV), f32),
            v((QN, LEV), f32), v((2 * KW, LEV), f32), v((2 * KW, LEV), f32),
            dma((3,)), dma((4,)), dma((4,)), dma((2,)), dma((4,)), dma((4,)), dma((1 + slots,)), dma((2,)),
            dma((STEPS, 2)), dma((STEPS, 2)), dma((1 + last,)), dma((2,)), dma((2,)), dma((2,)), dma, dma,
        ],
        compiler_params=pltpu.CompilerParams(
            collective_id=0, has_side_effects=True, vmem_limit_bytes=56 * 1024 * 1024),
    )(air.transpose(1, 0, 2), seaw, land, courant.reshape(1, LEV), vmix, cutoffs, inv, inva, ct, fold, wave)
    sea_out = sea_out[:, :, 0, :COLS].transpose(1, 0, 2).reshape(rp, nl * COLS)
    return air_out.transpose(1, 0, 2), sea_out


def solution(mesh):
    nl = mesh.shape["lon"]
    consts = tuple(jnp.asarray(x) for x in tables(nl))
    placed = (P("lat", "lon", None), P(("lat", "lon"), None), P("lat", "lon"), P(), P(), P())

    def run(*args):
        return jax.shard_map(
            functools.partial(local, nl),
            mesh=mesh,
            in_specs=((P(),) * 5,) + placed,
            out_specs=(P("lat", "lon", None), P(("lat", "lon"), None)),
            check_vma=False,
        )(consts, *args)

    return run
```

```python
import functools

import jax
import jax.numpy as jnp
import ml_dtypes
import numpy as np
from jax import lax
from jax.experimental import pallas as pl
from jax.experimental.pallas import tpu as pltpu
from jax.sharding import PartitionSpec as P

STEPS = 6
NPOLE = 16
ROWS = 32
COLS = 90
KW = 128
LEV = 128
HALO = 6
FRAMES = 49
WIDE = 120
Q0, QN = 8, 104
SPEC = NPOLE + HALO
GROUPS, GW = 6, 16
STARTS = (0, 15, 30, 45, 60, 74)

f32, bf16 = jnp.float32, jnp.bfloat16
MESH = pl.DeviceIdType.MESH


def split(x):
    hi = x.astype(bf16)
    return hi, (x - hi.astype(f32)).astype(bf16)


def dot(a, b):
    return jnp.dot(a, b, preferred_element_type=f32)


def dot3(a, b):
    return dot(a[0], b[0]) + dot(a[1], b[0]) + dot(a[0], b[1])


def dot3n(a, b):
    n = b[0].shape[1]
    both = dot(a[0], jnp.concatenate(b, 1))
    return both[:, :n] + both[:, n:] + dot(a[1], b[0])


def np_split(x):
    x = x.astype(np.float32)
    hi = x.astype(ml_dtypes.bfloat16)
    lo = (x - hi.astype(np.float32)).astype(ml_dtypes.bfloat16)
    return np.stack([hi, lo])


def tables(nl):
    nlon = nl * COLS
    kq = KW // nl
    k = (np.arange(nl)[:, None, None] * kq + np.arange(kq)[None, None, :]) * np.ones((1, 2, 1), int)
    sine = np.broadcast_to(np.arange(2)[None, :, None], k.shape).reshape(-1)
    k = k.reshape(-1)

    def fwd(c):
        ang = (c[..., None] * k % nlon) * (2.0 * np.pi / nlon)
        return np.where(sine == 0, np.cos(ang), np.sin(ang))

    d = np.arange(nl)[:, None]
    q = np.arange(QN)[None]
    weight = np.where(k == 0, 1.0, 2.0) / nlon
    inv = np.moveaxis(np_split(fwd((d * COLS + q - 8) % nlon) * weight), 0, 1)
    everywhere = np_split(fwd(np.arange(nl * COLS).reshape(nl, COLS)) * weight)
    packed = []
    for g in range(GROUPS):
        c = STARTS[g] + np.arange(GW)[None]
        ours = np.logical_and(c >= g * 15, c < g * 15 + 15)
        packed.append(np.where(ours[..., None], fwd(d * COLS + c), 0.0).reshape(nl * GW, 2 * KW).T)
    fold = np.zeros((LEV, 2 * LEV))
    for g in range(GROUPS):
        for r in range(SPEC - 1):
            fold[21 * g + r, r + 8] = 0.5
            for near in (r - 1, r + 1):
                if near >= 0:
                    fold[21 * g + r, LEV + near + 8] = 0.5
    fold = np.concatenate([fold, fold]).astype(ml_dtypes.bfloat16)
    step = 2.0 * np.pi / nlon
    wave = np.stack([0.6 + 0.2 * np.cos(k * step), np.where(sine == 0, -1.0, 1.0) * np.sin(k * step)])
    wave = np.broadcast_to(wave[:, :, None], (2, 2 * KW, LEV)).astype(np.float32)
    return inv, everywhere, np_split(np.concatenate(packed, 0)), fold, wave


def kernel(nl, a_hbm, sea_ref, land_ref, cour_ref, vmix_ref, cut_ref, inv_hbm, all_hbm, ct_hbm, fold_ref,
           wave_ref, out_hbm, seaout_ref, a_ref, out_ref, coef_ref, seaw_ref, fa, fb, sa, sb, rowb, spec, fx, fp, ex, ep, rs6, stage, fin, xs, xr, halo, coefr, sear,
           seab, seaf, seafin, sendx, recvx, inv, inva, ct, vb, mt, a0t, coeft, st0, st1, fluxt,
           at, keept, twice, vecs, tsem, asem, csem, seas, searow, xsem, rows, kss, fxs, exs, r6, fsem, xss, fins, isem, osem):
    lat, lon = lax.axis_index("lat"), lax.axis_index("lon")
    polar = jnp.logical_or(lat == 0, lat == 3)
    flip = lat == 3
    kq = KW // nl
    ko = 2 * kq
    rp = ROWS // nl
    half = nl // 2
    turn = lax.rem(lon, half) * 2 + lon // half
    lane = lax.broadcasted_iota(jnp.int32, (QN, LEV), 1)

    def natural(m):
        return jnp.where(flip, ROWS - 1 - m, m)

    def peers(body):
        here = lax.rem(lon, half)
        base = lon - here

        def across_half(i, carry):
            body(half - base + lax.rem(here + i, half))
            return carry

        def beside(i, carry):
            body(base + lax.rem(here + i, half))
            return carry
        lax.fori_loop(0, half, across_half, 0)
        lax.fori_loop(1, half, beside, 0)

    def wait_bytes(ref, sem):
        pltpu.make_async_copy(ref, ref, sem).wait()

    def to_lon(src, dst, ssem, rsem, peer):
        return pltpu.make_async_remote_copy(src, dst, ssem, rsem, device_id={"lon": peer},
                                            device_id_type=MESH)

    loads = [
        pltpu.make_async_copy(inv_hbm.at[lon], inv, tsem.at[0]),
        pltpu.make_async_copy(ct_hbm, ct, tsem.at[1]),
        pltpu.make_async_copy(all_hbm, inva, tsem.at[2]),
    ]

    @pl.when(polar)
    def _():
        for load in loads:
            load.start()

    rows_in = [pltpu.make_async_copy(a_hbm.at[:, m, :], a_ref.at[m], isem) for m in range(ROWS)]
    for row in rows_in:
        row.start()

    barrier = pltpu.get_barrier_semaphore()
    peers(lambda p: pl.semaphore_signal(barrier, inc=1, device_id={"lon": p}, device_id_type=MESH))

    @pl.when(lat < 3)
    def _():
        pl.semaphore_signal(barrier, inc=1, device_id={"lat": lat + 1}, device_id_type=MESH)

    @pl.when(lat > 0)
    def _():
        pl.semaphore_signal(barrier, inc=1, device_id={"lat": lat - 1}, device_id_type=MESH)

    pl.semaphore_wait(barrier, nl - 1 + jnp.where(polar, 1, 2))

    def own_coef(m, carry):
        coef_ref[m] = jnp.zeros((1, LEV), f32)
        coef_ref[m, :, pl.ds(0, COLS)] = jnp.where(land_ref[pl.ds(m, 1), :] == 1, 0.5, 0.15)
        return carry
    lax.fori_loop(0, ROWS, own_coef, 0)

    nlon = nl * COLS
    for d in range(nl):
        for i in range(rp):
            seaw_ref[d, i] = jnp.zeros((1, LEV), f32)
            lo, hi = d * COLS - 8, d * COLS + COLS + 8
            if lo < 0:
                seaw_ref[d, i, :, 0:8] = sea_ref[i:i + 1, nlon - 8:nlon]
                seaw_ref[d, i, :, 8:COLS + 16] = sea_ref[i:i + 1, 0:hi]
            elif hi > nlon:
                seaw_ref[d, i, :, 0:COLS + 8] = sea_ref[i:i + 1, lo:nlon]
                seaw_ref[d, i, :, COLS + 8:COLS + 16] = sea_ref[i:i + 1, 0:8]
            else:
                seaw_ref[d, i, :, 0:COLS + 16] = sea_ref[i:i + 1, lo:hi]
    wait_bytes(a_ref, isem)

    side = jnp.where(lat == 2, 1, 0)

    def lat_sends(src_ref, dst_ref, sems):
        def make(src, s, i, which, to):
            return pltpu.make_async_remote_copy(
                src_ref.at[src], dst_ref.at[s, i], sems.at[which], sems.at[2 + s],
                device_id={"lat": to}, device_id_type=MESH)

        @pl.when(lat < 3)
        def _():
            for i in range(HALO):
                make(jnp.where(lat == 2, ROWS - 1 - i, ROWS - HALO + i), side, i, 0, lat + 1).start()

        @pl.when(lat > 0)
        def _():
            for i in range(HALO):
                make(i, 1, i, 1, lat - 1).start()

    def lat_recvs(dst_ref, sems):
        wait_bytes(dst_ref.at[1], sems.at[3])

        @pl.when(jnp.logical_not(polar))
        def _():
            wait_bytes(dst_ref.at[0], sems.at[2])

    def lat_sent(dst_ref, sems):
        @pl.when(lat < 3)
        def _():
            wait_bytes(dst_ref.at[0], sems.at[0])

        @pl.when(lat > 0)
        def _():
            wait_bytes(dst_ref.at[0], sems.at[1])

    def owner(r):
        return (r % nl) % 2 * half + r % nl // 2

    @pl.when(polar)
    def _():
        for r in range(SPEC):
            @pl.when(lon != owner(r))
            def _():
                to_lon(a_ref.at[natural(r)], rowb.at[r // nl, lon], rows.at[0], rows.at[1 + r // nl], owner(r)).start()

    peers(lambda p: to_lon(seaw_ref.at[p], seab.at[pl.ds(rp * lon, rp)], seas.at[0], seas.at[1], p).start())
    lat_sends(coef_ref, coefr, csem)
    lat_sends(a_ref, halo, asem)

    @pl.when(polar)
    def _():
        for r in range(SPEC):
            @pl.when(lon == owner(r))
            def _():
                rowb[r // nl, lon] = a_ref[natural(r)]

    def own_sea(i, carry):
        seab[rp * lon + i] = seaw_ref[lon, i]
        return carry
    lax.fori_loop(0, rp, own_sea, 0)

    def clear(f, carry):
        z = jnp.zeros((8, LEV), f32)
        fa[f, pl.ds(0, 8), :] = z
        fa[f, pl.ds(WIDE - 16, 8), :] = z
        fa[f, pl.ds(WIDE - 8, 8), :] = z
        fb[f, pl.ds(0, 8), :] = z
        fb[f, pl.ds(WIDE - 8, 8), :] = z
        return carry
    lax.fori_loop(0, FRAMES, clear, 0)
    for f in (0, 1, 46, 47):
        fa[f] = jnp.zeros((WIDE, LEV), f32)
        fb[f] = jnp.zeros((WIDE, LEV), f32)
    fa[48] = jnp.zeros((WIDE, LEV), f32)
    fb[48] = jnp.zeros((WIDE, LEV), f32)

    def fill(m, carry):
        fa[m + 8, pl.ds(16, COLS), :] = a_ref[natural(m)]
        return carry
    lax.fori_loop(0, ROWS, fill, 0)

    col0 = jnp.broadcast_to(vmix_ref[:, 0:1], (LEV, LEV))
    rowid = lax.broadcasted_iota(jnp.int32, (LEV, LEV), 0)
    both = jnp.concatenate([vmix_ref[...], col0 + jnp.where(rowid == 0, 1.0, 0.0)], 1)
    bhi, blo = split(both)
    vb[0, pl.ds(0, LEV), :] = bhi
    vb[0, pl.ds(LEV, LEV), :] = bhi
    vb[1, pl.ds(0, LEV), :] = blo
    vb[1, pl.ds(LEV, LEV), :] = jnp.zeros_like(blo)

    def levels(x):
        both = jnp.concatenate(split(x), 1)
        res = dot(both, vb[0]) + dot(both, vb[1])
        return x + res[:, :LEV], res[:, LEV:]

    cour = cour_ref[...]
    east = 0.1 - 0.5 * cour
    west = 0.1 + 0.5 * cour
    lane1 = lax.broadcasted_iota(jnp.int32, (1, LEV), 1)
    vrow0 = vmix_ref[0:1, :] + jnp.where(lane1 == 0, 1.0, 0.0)
    half0 = jnp.where(lane1 == 0, 0.5, 0.0)
    kown = lon * kq + lax.rem(lax.broadcasted_iota(jnp.int32, (ko, LEV), 0), kq)
    olane = lax.broadcasted_iota(jnp.int32, (ko, LEV), 1)
    krow = lax.broadcasted_iota(jnp.int32, (2 * KW, LEV), 0)
    klane = lax.broadcasted_iota(jnp.int32, (2 * KW, LEV), 1)

    def swap(x, rowid):
        return jnp.where(lax.rem(rowid, ko) < kq, pltpu.roll(x, x.shape[0] - kq, 0), pltpu.roll(x, kq, 0))

    def cutoff(r):
        return cut_ref[jnp.where(flip, 2 * NPOLE - 1 - r, r)]

    mine = pl.ds(pl.multiple_of(lon * ko, 8), ko)

    @pl.when(polar)
    def _():
        cuts = jnp.full((1, LEV), KW, jnp.int32)
        for r in range(NPOLE):
            cuts = jnp.where(lane1 == r + 8, cutoff(r), cuts)
        kid = krow // ko * kq + lax.rem(krow, kq)
        keept[...] = jnp.where(kid <= cuts, 1.0, 0.0)
        pair = jnp.where(lax.broadcasted_iota(jnp.int32, (8, LEV), 0) == 0, 1.0, cour) * vrow0
        vecs[...] = levels(pair)[0]
        for buf in (sa, sb):
            buf[0] = jnp.zeros((ko, LEV), f32)
            buf[SPEC + 1] = jnp.zeros((ko, LEV), f32)

    lat_recvs(halo, asem)
    for i in range(HALO):
        fa[40 + i, pl.ds(16, COLS), :] = halo[1, i]

    @pl.when(jnp.logical_not(polar))
    def _():
        for i in range(HALO):
            fa[2 + i, pl.ds(16, COLS), :] = halo[0, i]

    @pl.when(polar)
    def _():
        for i in range(HALO):
            fa[2 + i] = jnp.zeros((WIDE, LEV), f32)
            fb[2 + i] = jnp.zeros((WIDE, LEV), f32)

    def gather_rows(own_of, got):
        mt[...] = jnp.zeros_like(mt)

        def put(m, carry):
            mt[pl.ds(m + 8, 1), :] = own_of(m)
            return carry
        lax.fori_loop(0, ROWS, put, 0)
        for i in range(HALO):
            mt[40 + i:41 + i, :] = got[1, i]

        @pl.when(jnp.logical_not(polar))
        def _():
            for i in range(HALO):
                mt[2 + i:3 + i, :] = got[0, i]
        return mt[...].T

    lat_recvs(coefr, csem)
    fa[48, pl.ds(16, COLS), :] = gather_rows(lambda m: coef_ref[natural(m)], coefr)[:COLS]

    def pack(f, carry):
        sendx[0, f] = fa[f, pl.ds(16 + COLS - 8, 8), :]
        sendx[1, f] = fa[f, pl.ds(16, 8), :]
        return carry
    lax.fori_loop(2, FRAMES, pack, 0)
    zero = jnp.zeros((8, LEV), f32)
    for s in range(2):
        for f in range(2):
            sendx[s, f] = zero
    ahead = lax.rem(lon + 1, nl)
    behind = lax.rem(lon + nl - 1, nl)
    to_east = to_lon(sendx.at[0], recvx.at[0], xsem.at[0], xsem.at[2], ahead)
    to_west = to_lon(sendx.at[1], recvx.at[1], xsem.at[1], xsem.at[3], behind)
    to_east.start()
    to_west.start()

    wait_bytes(seab.at[pl.ds(0, ROWS - rp)], seas.at[1])
    lat_sends(seab, sear, searow)

    def across(u, x):
        return lax.dot_general(u, x, (((1,), (1,)), ((), ())), preferred_element_type=f32)

    @pl.when(polar)
    def _():
        loads[0].wait()
        loads[1].wait()
        ident = jnp.where(rowid == lax.broadcasted_iota(jnp.int32, (LEV, LEV), 1), 1.0, 0.0)
        ucol = split((vmix_ref[...] + ident).T[0:8, :])
        for slot in range(-(-SPEC // nl)):
            r = slot * nl + turn

            @pl.when(r < SPEC)
            def _():
                wait_bytes(rowb.at[slot, pl.ds(0, nl - 1)], rows.at[1 + slot])
                acc = jnp.zeros((2 * KW, LEV), f32)
                for g in range(GROUPS):
                    cols = rowb[slot, :, pl.ds(STARTS[g], GW), :].reshape(nl * GW, LEV)
                    tab = (ct[0, pl.ds(2 * KW * g, 2 * KW), :], ct[1, pl.ds(2 * KW * g, 2 * KW), :])
                    acc = acc + dot3n(tab, split(cols))
                spec[slot] = acc
                waved = wave_ref[0] * acc + wave_ref[1] * cour * swap(acc, krow)
                pair = split(jnp.concatenate([waved, acc], 0))
                low = across(ucol[0], pair[0]) + across(ucol[1], pair[0]) + across(ucol[0], pair[1])
                for i in range(4):
                    xs[slot, i:i + 1, :] = low[0:1, i * LEV:(i + 1) * LEV]
                    xr[r, i:i + 1, :] = low[0:1, i * LEV:(i + 1) * LEV]
                peers(lambda p: to_lon(xs.at[slot], xr.at[r], xss.at[0], xss.at[1], p).start())

                def chunk(p):
                    return spec.at[slot, pl.ds(pl.multiple_of(p * ko, 8), ko)]
                peers(lambda p: to_lon(chunk(p), sa.at[r + 1], kss.at[0], kss.at[1], p).start())
                sa[r + 1] = spec[slot, mine, :]

    lat_recvs(sear, searow)
    st0[...] = jnp.zeros_like(st0)
    st1[...] = jnp.zeros_like(st1)
    st0[pl.ds(Q0, QN), :] = gather_rows(lambda m: seab[natural(m)], sear)[:QN]

    to_east.wait_recv()
    to_west.wait_recv()

    def unpack(f, carry):
        fa[f, pl.ds(8, 8), :] = recvx[0, f]
        fa[f, pl.ds(16 + COLS, 8), :] = recvx[1, f]
        return carry
    lax.fori_loop(2, FRAMES, unpack, 0)
    coeft[...] = fa[48, pl.ds(Q0, QN), :]

    def evolve(rows, src, dst, slot):
        wc = wave_ref[0, mine, :]
        ws = wave_ref[1, mine, :] * cour
        adv = []
        for r in range(rows):
            here = src[r + 1]
            x = wc * here + ws * swap(here, lax.broadcasted_iota(jnp.int32, (ko, LEV), 0)) + 0.1 * (src[r] + src[r + 2])
            adv.append(jnp.where(kown <= cutoff(r), x, 0.0) if r < NPOLE else x)
        new, low = levels(jnp.concatenate(adv, 0))
        if dst is not None:
            for r in range(rows):
                dst[r + 1] = new[r * ko:(r + 1) * ko]
        if slot is not None:
            level0 = jnp.zeros((ko, LEV), f32)
            for r in range(NPOLE):
                level0 = jnp.where(olane == r + 8, low[r * ko:(r + 1) * ko], level0)
            ep[slot, pl.ds(0, ko), :] = level0
            ep[slot, pl.ds(ko, ko), :] = new[(NPOLE - 1) * ko:NPOLE * ko]

    def message(got, made, sems, t):
        got[t, lon] = made[t]
        peers(lambda p: to_lon(made.at[t], got.at[t, lon], sems.at[t, 0], sems.at[t, 1], p).start())

    def message_wait(got, sems, t, which):
        wait_bytes(got.at[t, pl.ds(0, nl - 1)], sems.at[t, which])

    extra = turn < SPEC % nl

    def others_rows(ref, sem):
        @pl.when(extra)
        def _():
            wait_bytes(ref.at[pl.ds(0, SPEC - SPEC // nl - 1)], sem)

        @pl.when(jnp.logical_not(extra))
        def _():
            wait_bytes(ref.at[pl.ds(0, SPEC - SPEC // nl)], sem)

    def first_level0():
        others_rows(xr, xss.at[1])
        mt[...] = jnp.zeros_like(mt)
        cols = []
        for i in range(4):
            for r in range(NPOLE + 1):
                mt[r + 8:r + 9, :] = xr[r, i:i + 1, :]
            cols.append(mt[...].T)
        own, beside = jnp.concatenate(cols[:2], 0), jnp.concatenate(cols[2:], 0)
        near = pltpu.roll(beside, 1, 1) + pltpu.roll(beside, LEV - 1, 1)
        return (own + 0.1 * near) * keept[...]

    def last_rows():
        loads[2].wait()
        here = lax.rem(lon, half)
        base = lon - here
        for slot in range(NPOLE // half):
            r = slot * half + here
            wait_bytes(rs6.at[slot, pl.ds(0, nl - 1)], r6.at[1 + slot])
            waves = split(rs6[slot].reshape(2 * KW, LEV))

            def one(i, carry):
                at_i = lax.rem(here + i, half)
                p = base + at_i
                stage[slot, at_i] = dot3n((inva[0, p], inva[1, p]), waves)
                to_lon(stage.at[slot, at_i], fin.at[r], fsem.at[0], fsem.at[1], p).start()
                return carry
            lax.fori_loop(1, half, one, 0)
            fin[r] = dot3n((inva[0, lon], inva[1, lon]), waves)

    lane_ok = jnp.logical_or(lane >= 8, jnp.logical_not(polar))
    glane = lax.broadcasted_iota(jnp.int32, (GW, LEV), 1) // 21

    for t in range(1, STEPS + 1):
        src, dst = (fa, fb) if t % 2 else (fb, fa)
        sprev, snow = (sa, sb) if t % 2 else (sb, sa)
        sea, sea_next = (st0, st1) if t % 2 else (st1, st0)
        first = jnp.where(polar, 8 + NPOLE, 2 + t)
        count = jnp.where(polar, -(-(22 - t) // 4), -(-(44 - 2 * t) // 4))

        def grid_rows(i, acc):
            adv = []
            for j in range(4):
                f = first + 4 * i + j
                mid = pl.ds(Q0, QN)
                adv.append(0.6 * src[f, mid, :] + 0.1 * (src[f - 1, mid, :] + src[f + 1, mid, :])
                           + east * src[f, pl.ds(Q0 + 1, QN), :] + west * src[f, pl.ds(Q0 - 1, QN), :])
            new, low = levels(jnp.concatenate(adv, 0))
            for j in range(4):
                f = first + 4 * i + j
                dst[f, pl.ds(Q0, QN), :] = new[j * QN:(j + 1) * QN]
                acc = jnp.where(lane == f, low[j * QN:(j + 1) * QN], acc)
            return acc
        a0t[...] = lax.fori_loop(0, count, grid_rows, jnp.zeros((QN, LEV), f32))

        @pl.when(polar)
        def _():
            if t == STEPS:
                last_rows()
            if t > 1:
                message_wait(fx, fxs, t - 1, 1)
                got = split(fx[t - 1].reshape(nl * GW, LEV))
                res = jnp.zeros((2 * KW, LEV), f32)
                for g in range(GROUPS):
                    tab = (ct[0, pl.ds(2 * KW * g, 2 * KW), :], ct[1, pl.ds(2 * KW * g, 2 * KW), :])
                    res = jnp.where(klane // 21 == g, dot3n(tab, got), res)
                hats = dot(jnp.concatenate(split(res), 1), fold_ref[...])
                hat, near = hats[:, :LEV], hats[:, LEV:]
                add = wave_ref[0] * hat + wave_ref[1] * cour[:, 0:1] * swap(hat, krow) + 0.1 * near
                add = add * keept[...]
                at[...] = add
            if t == 1:
                res = dot3n((inv[0], inv[1]), split(first_level0()))
            else:
                message_wait(ex, exs, t - 1, 1)
                level0 = ex[t - 1, :, pl.ds(0, ko), :].reshape(2 * KW, LEV) + vrow0[:, 0:1] * add
                edge = ex[t - 1, :, pl.ds(ko, ko), :].reshape(2 * KW, LEV)
                if t > 2:
                    for i in range(2):
                        vec = vecs[i:i + 1, :]
                        level0 = level0 + vec[:, 0:1] * twice[i]
                        edge = edge + twice[i][:, 7 + NPOLE:8 + NPOLE] * vec
                edge = edge + add[:, 7 + NPOLE:8 + NPOLE] * vrow0 if t < STEPS else add
                res = dot3((inv[0], inv[1]), split(jnp.concatenate([level0, edge], 1)))
            filtered = jnp.logical_and(lane >= 8, lane < 8 + NPOLE)
            a0t[...] = jnp.where(filtered, res[:, :LEV], a0t[...])
            if t == STEPS:
                at[pl.ds(0, QN), :] = res[:, LEV:]
            elif t > 1:
                dst[7 + NPOLE, pl.ds(Q0, QN), :] = res[:, LEV:]

        now = sea[pl.ds(Q0, QN), :]
        flux = coeft[...] * (now - a0t[...])
        fluxt[...] = flux

        if t < STEPS:
            @pl.when(polar)
            def _():
                msg = jnp.zeros((GW, LEV), f32)
                for g in range(GROUPS):
                    turned = pltpu.roll(fluxt[pl.ds(8 + STARTS[g], GW), :], (21 * g - 8) % LEV, 1)
                    msg = jnp.where(glane == g, turned, msg)
                fp[t] = msg
                message(fx, fp, fxs, t)
                if t == 1:
                    others_rows(sa, kss.at[1])
                    evolve(SPEC - 1, sa, sb, 0)
                    message(ex, ep, exs, 0)
                else:
                    own = at[mine, :]
                    for r in range(SPEC - t):
                        snow[r + 1] = snow[r + 1] + own[:, r + 8:r + 9] * vrow0
                evolve(SPEC - 1 - t, snow, sprev, 1 if t == 1 else None)
                if t == 1:
                    message(ex, ep, exs, 1)
                if t < STEPS - 1:
                    evolve(NPOLE, sprev, None, t + 1)
                    message(ex, ep, exs, t + 1)
                if 1 < t:
                    add = at[...]
                    near = pltpu.roll(add, 1, 1) + pltpu.roll(add, LEV - 1, 1)
                    twice[0] = (wave_ref[0] * add + 0.1 * near) * keept[...]
                    twice[1] = wave_ref[1] * swap(add, krow) * keept[...]
                if t == STEPS - 1:
                    for r in range(NPOLE):
                        for dev in (r % half, half + r % half):
                            @pl.when(lon != dev)
                            def _():
                                to_lon(sprev.at[r + 1], rs6.at[r // half, lon], r6.at[0], r6.at[1 + r // half], dev).start()

                            @pl.when(lon == dev)
                            def _():
                                rs6[r // half, lon] = sprev[r + 1]

        around = (pltpu.roll(now, 1, 1) + pltpu.roll(now, LEV - 1, 1)
                  + sea[pl.ds(Q0 - 1, QN), :] + sea[pl.ds(Q0 + 1, QN), :])
        later = now - 0.3 * flux + 0.2 * (around - 4.0 * now)
        sea_next[pl.ds(Q0, QN), :] = jnp.where(lane_ok, later, 0.0)

        if t == 1:
            @pl.when(polar)
            def _():
                message_wait(ex, exs, 0, 1)
                edge = ex[0, :, pl.ds(ko, ko), :].reshape(2 * KW, LEV)
                dst[7 + NPOLE, pl.ds(Q0, QN), :] = dot3n((inv[0], inv[1]), split(edge))

        def warm(f):
            dst[f, pl.ds(Q0, QN), :] = dst[f, pl.ds(Q0, QN), :] + fluxt[:, f:f + 1] * half0

        def warm_all():
            @pl.when(jnp.logical_not(polar))
            def _():
                for f in range(2 + t, 7 + NPOLE):
                    warm(f)
            for f in range(7 + NPOLE, 46 - t):
                warm(f)
        if t < STEPS:
            warm_all()

    last, sea = fa, st0

    mt[...] = sea[pl.ds(16, LEV), :].T

    def put_row(n, carry):
        seaf[n] = mt[pl.ds(natural(n) + 8, 1), :]
        return carry
    lax.fori_loop(0, ROWS, put_row, 0)
    peers(lambda p: to_lon(seaf.at[pl.ds(rp * p, rp)], seafin.at[lon], fins.at[0], fins.at[1], p).start())

    def own_fin(i, carry):
        seafin[lon, i] = seaf[rp * lon + i]
        return carry
    lax.fori_loop(0, rp, own_fin, 0)

    warm_all()

    def give_grid(m, carry):
        out_ref[natural(m)] = last[m + 8, pl.ds(16, COLS), :]
        return carry
    lax.fori_loop(jnp.where(polar, NPOLE, 0), ROWS, give_grid, 0)

    def row_out(m):
        n = natural(m)
        pltpu.make_async_copy(out_ref.at[n], out_hbm.at[:, n, :], osem).start()

    for m in range(NPOLE, ROWS):
        row_out(m)

    @pl.when(jnp.logical_not(polar))
    def _():
        for m in range(NPOLE):
            row_out(m)

    @pl.when(polar)
    def _():
        wait_bytes(fin.at[pl.ds(0, NPOLE - NPOLE // half)], fsem.at[1])
        for r in range(NPOLE):
            out_ref[natural(r)] = (fin[r] + at[pl.ds(8, COLS), r + 8:r + 9] * vrow0
                                   + fluxt[pl.ds(8, COLS), r + 8:r + 9] * half0)
            row_out(r)

    wait_bytes(seafin.at[pl.ds(0, nl - 1)], fins.at[1])
    for d in range(nl):
        for i in range(rp):
            seaout_ref[i:i + 1, d * COLS:d * COLS + COLS] = seafin[d, i, :, 0:COLS]

    wait_bytes(out_ref, osem)
    wait_bytes(seafin.at[pl.ds(0, nl - 1)], fins.at[0])
    wait_bytes(seab.at[pl.ds(0, ROWS - rp)], seas.at[0])
    lat_sent(halo, asem)
    lat_sent(coefr, csem)
    lat_sent(sear, searow)
    to_east.wait_send()
    to_west.wait_send()

    @pl.when(polar)
    def _():
        for r in range(SPEC):
            @pl.when(lon != owner(r))
            def _():
                wait_bytes(a_ref.at[0], rows.at[0])
        for slot in range(-(-SPEC // nl)):
            @pl.when(slot * nl + turn < SPEC)
            def _():
                wait_bytes(spec.at[slot, pl.ds(0, (nl - 1) * ko)], kss.at[0])
                peers(lambda p: wait_bytes(xs.at[slot], xss.at[0]))
        for t in range(STEPS):
            message_wait(ex, exs, t, 0)
        for t in range(1, STEPS):
            message_wait(fx, fxs, t, 0)
        for r in range(NPOLE):
            for dev in (r % half, half + r % half):
                @pl.when(lon != dev)
                def _():
                    wait_bytes(sa.at[0], r6.at[0])
        for slot in range(NPOLE // half):
            wait_bytes(stage.at[slot, pl.ds(0, half - 1)], fsem.at[0])


def local(nl, consts, air, sea, land, courant, vmix, cutoffs):
    rp = ROWS // nl
    ko = 2 * KW // nl
    inv, inva, ct, fold, wave = consts
    half = nl // 2
    last = NPOLE // half
    slots = -(-SPEC // nl)
    vm = pl.BlockSpec(memory_space=pltpu.VMEM)
    hbm = pl.BlockSpec(memory_space=pl.ANY)
    dma = pltpu.SemaphoreType.DMA
    v = pltpu.VMEM
    air_out, sea_out = pl.pallas_call(
        functools.partial(kernel, nl),
        out_shape=(jax.ShapeDtypeStruct((COLS, ROWS, LEV), f32),
                   jax.ShapeDtypeStruct((rp, nl * COLS), f32)),
        in_specs=[hbm, vm, vm, vm, vm, pl.BlockSpec(memory_space=pltpu.SMEM), hbm, hbm, hbm, vm, vm],
        out_specs=(hbm, vm),
        scratch_shapes=[
            v((ROWS, COLS, LEV), f32), v((ROWS, COLS, LEV), f32), v((ROWS, 1, LEV), f32), v((nl, rp, 1, LEV), f32),
            v((FRAMES, WIDE, LEV), f32), v((FRAMES, WIDE, LEV), f32),
            v((SPEC + 2, ko, LEV), f32), v((SPEC + 2, ko, LEV), f32),
            v((slots, nl, COLS, LEV), f32), v((slots, 2 * KW, LEV), f32),
            v((STEPS, nl, GW, LEV), f32), v((STEPS, GW, LEV), f32),
            v((STEPS, nl, 2 * ko, LEV), f32), v((STEPS, 2 * ko, LEV), f32),
            v((last, nl, ko, LEV), f32), v((last, half, COLS, LEV), f32), v((NPOLE, COLS, LEV), f32),
            v((slots, 4, LEV), f32), v((SPEC, 4, LEV), f32),
            v((2, HALO, COLS, LEV), f32), v((2, HALO, 1, LEV), f32), v((2, HALO, 1, LEV), f32),
            v((ROWS, 1, LEV), f32), v((ROWS, 1, LEV), f32), v((nl, rp, 1, LEV), f32),
            v((2, FRAMES, 8, LEV), f32), v((2, FRAMES, 8, LEV), f32),
            v((2, QN, 2 * KW), bf16), v((2, nl, COLS, 2 * KW), bf16), v((2, GROUPS * 2 * KW, nl * GW), bf16),
            v((2, 2 * LEV, 2 * LEV), bf16), v((LEV, LEV), f32),
            v((QN, LEV), f32), v((QN, LEV), f32), v((144, LEV), f32), v((144, LEV), f32),
            v((QN, LEV), f32), v((2 * KW, LEV), f32), v((2 * KW, LEV), f32), v((2, 2 * KW, LEV), f32), v((8, LEV), f32),
            dma((3,)), dma((4,)), dma((4,)), dma((2,)), dma((4,)), dma((4,)), dma((1 + slots,)), dma((2,)),
            dma((STEPS, 2)), dma((STEPS, 2)), dma((1 + last,)), dma((2,)), dma((2,)), dma((2,)), dma, dma,
        ],
        compiler_params=pltpu.CompilerParams(
            collective_id=0, has_side_effects=True, vmem_limit_bytes=56 * 1024 * 1024),
    )(air.transpose(1, 0, 2), sea, land, courant.reshape(1, LEV), vmix, cutoffs, inv, inva, ct, fold, wave)
    return air_out.transpose(1, 0, 2), sea_out


def solution(mesh):
    nl = mesh.shape["lon"]
    consts = tuple(jnp.asarray(x) for x in tables(nl))
    placed = (P("lat", "lon", None), P(("lat", "lon"), None), P("lat", "lon"), P(), P(), P())

    def run(*args):
        return jax.shard_map(
            functools.partial(local, nl),
            mesh=mesh,
            in_specs=((P(),) * 5,) + placed,
            out_specs=(P("lat", "lon", None), P(("lat", "lon"), None)),
            check_vma=False,
        )(consts, *args)

    return run
```

```python
import functools

import jax
import jax.numpy as jnp
import ml_dtypes
import numpy as np
from jax import lax
from jax.experimental import pallas as pl
from jax.experimental.pallas import tpu as pltpu
from jax.sharding import PartitionSpec as P

STEPS = 6
NPOLE = 16
ROWS = 32
COLS = 90
KW = 128
LEV = 128
HALO = 6
FRAMES = 49
WIDE = 120
Q0, QN = 8, 104
SPEC = NPOLE + HALO
GROUPS, GW = 6, 16
STARTS = (0, 15, 30, 45, 60, 74)

f32, bf16 = jnp.float32, jnp.bfloat16
MESH = pl.DeviceIdType.MESH


def split(x):
    hi = x.astype(bf16)
    return hi, (x - hi.astype(f32)).astype(bf16)


def dot(a, b):
    return jnp.dot(a, b, preferred_element_type=f32)


def dot3(a, b):
    return dot(a[0], b[0]) + dot(a[1], b[0]) + dot(a[0], b[1])


def dot3n(a, b):
    n = b[0].shape[1]
    both = dot(a[0], jnp.concatenate(b, 1))
    return both[:, :n] + both[:, n:] + dot(a[1], b[0])


def np_split(x):
    x = x.astype(np.float32)
    hi = x.astype(ml_dtypes.bfloat16)
    lo = (x - hi.astype(np.float32)).astype(ml_dtypes.bfloat16)
    return np.stack([hi, lo])


def tables(nl):
    nlon = nl * COLS
    kq = KW // nl
    k = (np.arange(nl)[:, None, None] * kq + np.arange(kq)[None, None, :]) * np.ones((1, 2, 1), int)
    sine = np.broadcast_to(np.arange(2)[None, :, None], k.shape).reshape(-1)
    k = k.reshape(-1)

    def fwd(c):
        ang = (c[..., None] * k % nlon) * (2.0 * np.pi / nlon)
        return np.where(sine == 0, np.cos(ang), np.sin(ang))

    d = np.arange(nl)[:, None]
    q = np.arange(QN)[None]
    weight = np.where(k == 0, 1.0, 2.0) / nlon
    inv = np.moveaxis(np_split(fwd((d * COLS + q - 8) % nlon) * weight), 0, 1)
    everywhere = np_split(fwd(np.arange(nl * COLS).reshape(nl, COLS)) * weight)
    packed = []
    for g in range(GROUPS):
        c = STARTS[g] + np.arange(GW)[None]
        ours = np.logical_and(c >= g * 15, c < g * 15 + 15)
        packed.append(np.where(ours[..., None], fwd(d * COLS + c), 0.0).reshape(nl * GW, 2 * KW).T)
    fold = np.zeros((LEV, 2 * LEV))
    for g in range(GROUPS):
        for r in range(SPEC - 1):
            fold[21 * g + r, r + 8] = 0.5
            for near in (r - 1, r + 1):
                if near >= 0:
                    fold[21 * g + r, LEV + near + 8] = 0.5
    fold = np.concatenate([fold, fold]).astype(ml_dtypes.bfloat16)
    step = 2.0 * np.pi / nlon
    wave = np.stack([0.6 + 0.2 * np.cos(k * step), np.where(sine == 0, -1.0, 1.0) * np.sin(k * step)])
    wave = np.broadcast_to(wave[:, :, None], (2, 2 * KW, LEV)).astype(np.float32)
    return inv, everywhere, np_split(np.concatenate(packed, 0)), fold, wave


def kernel(nl, a_hbm, sea_ref, land_ref, cour_ref, vmix_ref, cut_ref, inv_hbm, all_hbm, ct_hbm, fold_ref,
           wave_ref, out_hbm, seaout_ref, a_ref, out_ref, coef_ref, seaw_ref, fa, fb, sa, sb, rowb, spec, fx, fp, ex, ep, rs6, stage, fin, xs, xr, halo, coefr, sear,
           seab, seaf, seafin, sendx, recvx, inv, inva, ct, vb, mt, a0t, coeft, st0, st1, fluxt,
           at, keept, twice, vecs, tsem, asem, csem, seas, searow, xsem, rows, kss, fxs, exs, r6, fsem, xss, fins, isem, osem):
    lat, lon = lax.axis_index("lat"), lax.axis_index("lon")
    polar = jnp.logical_or(lat == 0, lat == 3)
    flip = lat == 3
    kq = KW // nl
    ko = 2 * kq
    rp = ROWS // nl
    half = nl // 2
    turn = lax.rem(lon, half) * 2 + lon // half
    lane = lax.broadcasted_iota(jnp.int32, (QN, LEV), 1)

    def natural(m):
        return jnp.where(flip, ROWS - 1 - m, m)

    def peers(body):
        here = lax.rem(lon, half)
        base = lon - here

        def across_half(i, carry):
            body(half - base + lax.rem(here + i, half))
            return carry

        def beside(i, carry):
            body(base + lax.rem(here + i, half))
            return carry
        lax.fori_loop(0, half, across_half, 0)
        lax.fori_loop(1, half, beside, 0)

    def wait_bytes(ref, sem):
        pltpu.make_async_copy(ref, ref, sem).wait()

    def to_lon(src, dst, ssem, rsem, peer):
        return pltpu.make_async_remote_copy(src, dst, ssem, rsem, device_id={"lon": peer},
                                            device_id_type=MESH)

    loads = [
        pltpu.make_async_copy(inv_hbm.at[lon], inv, tsem.at[0]),
        pltpu.make_async_copy(ct_hbm, ct, tsem.at[1]),
        pltpu.make_async_copy(all_hbm, inva, tsem.at[2]),
    ]

    @pl.when(polar)
    def _():
        for load in loads:
            load.start()

    rows_in = [pltpu.make_async_copy(a_hbm.at[:, m, :], a_ref.at[m], isem) for m in range(ROWS)]
    for row in rows_in:
        row.start()

    barrier = pltpu.get_barrier_semaphore()
    peers(lambda p: pl.semaphore_signal(barrier, inc=1, device_id={"lon": p}, device_id_type=MESH))

    @pl.when(lat < 3)
    def _():
        pl.semaphore_signal(barrier, inc=1, device_id={"lat": lat + 1}, device_id_type=MESH)

    @pl.when(lat > 0)
    def _():
        pl.semaphore_signal(barrier, inc=1, device_id={"lat": lat - 1}, device_id_type=MESH)

    pl.semaphore_wait(barrier, nl - 1 + jnp.where(polar, 1, 2))

    def own_coef(m, carry):
        coef_ref[m] = jnp.zeros((1, LEV), f32)
        coef_ref[m, :, pl.ds(0, COLS)] = jnp.where(land_ref[pl.ds(m, 1), :] == 1, 0.5, 0.15)
        return carry
    lax.fori_loop(0, ROWS, own_coef, 0)

    nlon = nl * COLS
    for d in range(nl):
        for i in range(rp):
            seaw_ref[d, i] = jnp.zeros((1, LEV), f32)
            lo, hi = d * COLS - 8, d * COLS + COLS + 8
            if lo < 0:
                seaw_ref[d, i, :, 0:8] = sea_ref[i:i + 1, nlon - 8:nlon]
                seaw_ref[d, i, :, 8:COLS + 16] = sea_ref[i:i + 1, 0:hi]
            elif hi > nlon:
                seaw_ref[d, i, :, 0:COLS + 8] = sea_ref[i:i + 1, lo:nlon]
                seaw_ref[d, i, :, COLS + 8:COLS + 16] = sea_ref[i:i + 1, 0:8]
            else:
                seaw_ref[d, i, :, 0:COLS + 16] = sea_ref[i:i + 1, lo:hi]
    wait_bytes(a_ref, isem)

    side = jnp.where(lat == 2, 1, 0)

    def lat_sends(src_ref, dst_ref, sems):
        def make(src, s, i, which, to):
            return pltpu.make_async_remote_copy(
                src_ref.at[src], dst_ref.at[s, i], sems.at[which], sems.at[2 + s],
                device_id={"lat": to}, device_id_type=MESH)

        @pl.when(lat < 3)
        def _():
            for i in range(HALO):
                make(jnp.where(lat == 2, ROWS - 1 - i, ROWS - HALO + i), side, i, 0, lat + 1).start()

        @pl.when(lat > 0)
        def _():
            for i in range(HALO):
                make(i, 1, i, 1, lat - 1).start()

    def lat_recvs(dst_ref, sems):
        wait_bytes(dst_ref.at[1], sems.at[3])

        @pl.when(jnp.logical_not(polar))
        def _():
            wait_bytes(dst_ref.at[0], sems.at[2])

    def lat_sent(dst_ref, sems):
        @pl.when(lat < 3)
        def _():
            wait_bytes(dst_ref.at[0], sems.at[0])

        @pl.when(lat > 0)
        def _():
            wait_bytes(dst_ref.at[0], sems.at[1])

    def owner(r):
        return (r % nl) % 2 * half + r % nl // 2

    @pl.when(polar)
    def _():
        def send_row(i, carry):
            r = lax.rem(lon + i, SPEC)
            slot, w = lax.div(r, nl), lax.rem(r, nl)
            dev = lax.rem(w, 2) * half + lax.div(w, 2)

            @pl.when(lon != dev)
            def _():
                to_lon(a_ref.at[natural(r)], rowb.at[slot, lon], rows.at[0], rows.at[1 + slot], dev).start()
            return carry
        lax.fori_loop(0, SPEC, send_row, 0)

    peers(lambda p: to_lon(seaw_ref.at[p], seab.at[pl.ds(rp * lon, rp)], seas.at[0], seas.at[1], p).start())
    lat_sends(coef_ref, coefr, csem)
    lat_sends(a_ref, halo, asem)

    @pl.when(polar)
    def _():
        for r in range(SPEC):
            @pl.when(lon == owner(r))
            def _():
                rowb[r // nl, lon] = a_ref[natural(r)]

    def own_sea(i, carry):
        seab[rp * lon + i] = seaw_ref[lon, i]
        return carry
    lax.fori_loop(0, rp, own_sea, 0)

    def clear(f, carry):
        z = jnp.zeros((8, LEV), f32)
        fa[f, pl.ds(0, 8), :] = z
        fa[f, pl.ds(WIDE - 16, 8), :] = z
        fa[f, pl.ds(WIDE - 8, 8), :] = z
        fb[f, pl.ds(0, 8), :] = z
        fb[f, pl.ds(WIDE - 8, 8), :] = z
        return carry
    lax.fori_loop(0, FRAMES, clear, 0)
    for f in (0, 1, 46, 47):
        fa[f] = jnp.zeros((WIDE, LEV), f32)
        fb[f] = jnp.zeros((WIDE, LEV), f32)
    fa[48] = jnp.zeros((WIDE, LEV), f32)
    fb[48] = jnp.zeros((WIDE, LEV), f32)

    def fill(m, carry):
        fa[m + 8, pl.ds(16, COLS), :] = a_ref[natural(m)]
        return carry
    lax.fori_loop(0, ROWS, fill, 0)

    col0 = jnp.broadcast_to(vmix_ref[:, 0:1], (LEV, LEV))
    rowid = lax.broadcasted_iota(jnp.int32, (LEV, LEV), 0)
    both = jnp.concatenate([vmix_ref[...], col0 + jnp.where(rowid == 0, 1.0, 0.0)], 1)
    bhi, blo = split(both)
    vb[0, pl.ds(0, LEV), :] = bhi
    vb[0, pl.ds(LEV, LEV), :] = bhi
    vb[1, pl.ds(0, LEV), :] = blo
    vb[1, pl.ds(LEV, LEV), :] = jnp.zeros_like(blo)

    def levels(x):
        both = jnp.concatenate(split(x), 1)
        res = dot(both, vb[0]) + dot(both, vb[1])
        return x + res[:, :LEV], res[:, LEV:]

    cour = cour_ref[...]
    east = 0.1 - 0.5 * cour
    west = 0.1 + 0.5 * cour
    lane1 = lax.broadcasted_iota(jnp.int32, (1, LEV), 1)
    vrow0 = vmix_ref[0:1, :] + jnp.where(lane1 == 0, 1.0, 0.0)
    half0 = jnp.where(lane1 == 0, 0.5, 0.0)
    kown = lon * kq + lax.rem(lax.broadcasted_iota(jnp.int32, (ko, LEV), 0), kq)
    olane = lax.broadcasted_iota(jnp.int32, (ko, LEV), 1)
    krow = lax.broadcasted_iota(jnp.int32, (2 * KW, LEV), 0)
    klane = lax.broadcasted_iota(jnp.int32, (2 * KW, LEV), 1)

    def swap(x, rowid):
        return jnp.where(lax.rem(rowid, ko) < kq, pltpu.roll(x, x.shape[0] - kq, 0), pltpu.roll(x, kq, 0))

    def cutoff(r):
        return cut_ref[jnp.where(flip, 2 * NPOLE - 1 - r, r)]

    mine = pl.ds(pl.multiple_of(lon * ko, 8), ko)

    @pl.when(polar)
    def _():
        cuts = jnp.full((1, LEV), KW, jnp.int32)
        for r in range(NPOLE):
            cuts = jnp.where(lane1 == r + 8, cutoff(r), cuts)
        kid = krow // ko * kq + lax.rem(krow, kq)
        keept[...] = jnp.where(kid <= cuts, 1.0, 0.0)
        pair = jnp.where(lax.broadcasted_iota(jnp.int32, (8, LEV), 0) == 0, 1.0, cour) * vrow0
        vecs[...] = levels(pair)[0]
        for buf in (sa, sb):
            buf[0] = jnp.zeros((ko, LEV), f32)
            buf[SPEC + 1] = jnp.zeros((ko, LEV), f32)

    lat_recvs(halo, asem)
    for i in range(HALO):
        fa[40 + i, pl.ds(16, COLS), :] = halo[1, i]

    @pl.when(jnp.logical_not(polar))
    def _():
        for i in range(HALO):
            fa[2 + i, pl.ds(16, COLS), :] = halo[0, i]

    @pl.when(polar)
    def _():
        for i in range(HALO):
            fa[2 + i] = jnp.zeros((WIDE, LEV), f32)
            fb[2 + i] = jnp.zeros((WIDE, LEV), f32)

    def gather_rows(own_of, got):
        mt[...] = jnp.zeros_like(mt)

        def put(m, carry):
            mt[pl.ds(m + 8, 1), :] = own_of(m)
            return carry
        lax.fori_loop(0, ROWS, put, 0)
        for i in range(HALO):
            mt[40 + i:41 + i, :] = got[1, i]

        @pl.when(jnp.logical_not(polar))
        def _():
            for i in range(HALO):
                mt[2 + i:3 + i, :] = got[0, i]
        return mt[...].T

    lat_recvs(coefr, csem)
    fa[48, pl.ds(16, COLS), :] = gather_rows(lambda m: coef_ref[natural(m)], coefr)[:COLS]

    def pack(f, carry):
        sendx[0, f] = fa[f, pl.ds(16 + COLS - 8, 8), :]
        sendx[1, f] = fa[f, pl.ds(16, 8), :]
        return carry
    lax.fori_loop(2, FRAMES, pack, 0)
    zero = jnp.zeros((8, LEV), f32)
    for s in range(2):
        for f in range(2):
            sendx[s, f] = zero
    ahead = lax.rem(lon + 1, nl)
    behind = lax.rem(lon + nl - 1, nl)
    to_east = to_lon(sendx.at[0], recvx.at[0], xsem.at[0], xsem.at[2], ahead)
    to_west = to_lon(sendx.at[1], recvx.at[1], xsem.at[1], xsem.at[3], behind)
    to_east.start()
    to_west.start()

    wait_bytes(seab.at[pl.ds(0, ROWS - rp)], seas.at[1])
    lat_sends(seab, sear, searow)

    def across(u, x):
        return lax.dot_general(u, x, (((1,), (1,)), ((), ())), preferred_element_type=f32)

    @pl.when(polar)
    def _():
        loads[0].wait()
        loads[1].wait()
        ident = jnp.where(rowid == lax.broadcasted_iota(jnp.int32, (LEV, LEV), 1), 1.0, 0.0)
        ucol = split((vmix_ref[...] + ident).T[0:8, :])
        for slot in range(-(-SPEC // nl)):
            r = slot * nl + turn

            @pl.when(r < SPEC)
            def _():
                wait_bytes(rowb.at[slot, pl.ds(0, nl - 1)], rows.at[1 + slot])
                acc = jnp.zeros((2 * KW, LEV), f32)
                for g in range(GROUPS):
                    cols = rowb[slot, :, pl.ds(STARTS[g], GW), :].reshape(nl * GW, LEV)
                    tab = (ct[0, pl.ds(2 * KW * g, 2 * KW), :], ct[1, pl.ds(2 * KW * g, 2 * KW), :])
                    acc = acc + dot3n(tab, split(cols))
                spec[slot] = acc
                waved = wave_ref[0] * acc + wave_ref[1] * cour * swap(acc, krow)
                pair = split(jnp.concatenate([waved, acc], 0))
                low = across(ucol[0], pair[0]) + across(ucol[1], pair[0]) + across(ucol[0], pair[1])
                for i in range(4):
                    xs[slot, i:i + 1, :] = low[0:1, i * LEV:(i + 1) * LEV]
                    xr[r, i:i + 1, :] = low[0:1, i * LEV:(i + 1) * LEV]
                peers(lambda p: to_lon(xs.at[slot], xr.at[r], xss.at[0], xss.at[1], p).start())

                def chunk(p):
                    return spec.at[slot, pl.ds(pl.multiple_of(p * ko, 8), ko)]
                peers(lambda p: to_lon(chunk(p), sa.at[r + 1], kss.at[0], kss.at[1], p).start())
                sa[r + 1] = spec[slot, mine, :]

    lat_recvs(sear, searow)
    st0[...] = jnp.zeros_like(st0)
    st1[...] = jnp.zeros_like(st1)
    st0[pl.ds(Q0, QN), :] = gather_rows(lambda m: seab[natural(m)], sear)[:QN]

    to_east.wait_recv()
    to_west.wait_recv()

    def unpack(f, carry):
        fa[f, pl.ds(8, 8), :] = recvx[0, f]
        fa[f, pl.ds(16 + COLS, 8), :] = recvx[1, f]
        return carry
    lax.fori_loop(2, FRAMES, unpack, 0)
    coeft[...] = fa[48, pl.ds(Q0, QN), :]

    def evolve(rows, src, dst, slot):
        wc = wave_ref[0, mine, :]
        ws = wave_ref[1, mine, :] * cour
        adv = []
        for r in range(rows):
            here = src[r + 1]
            x = wc * here + ws * swap(here, lax.broadcasted_iota(jnp.int32, (ko, LEV), 0)) + 0.1 * (src[r] + src[r + 2])
            adv.append(jnp.where(kown <= cutoff(r), x, 0.0) if r < NPOLE else x)
        new, low = levels(jnp.concatenate(adv, 0))
        if dst is not None:
            for r in range(rows):
                dst[r + 1] = new[r * ko:(r + 1) * ko]
        if slot is not None:
            level0 = jnp.zeros((ko, LEV), f32)
            for r in range(NPOLE):
                level0 = jnp.where(olane == r + 8, low[r * ko:(r + 1) * ko], level0)
            ep[slot, pl.ds(0, ko), :] = level0
            ep[slot, pl.ds(ko, ko), :] = new[(NPOLE - 1) * ko:NPOLE * ko]

    def message(got, made, sems, t):
        got[t, lon] = made[t]
        peers(lambda p: to_lon(made.at[t], got.at[t, lon], sems.at[t, 0], sems.at[t, 1], p).start())

    def message_wait(got, sems, t, which):
        wait_bytes(got.at[t, pl.ds(0, nl - 1)], sems.at[t, which])

    extra = turn < SPEC % nl

    def others_rows(ref, sem):
        @pl.when(extra)
        def _():
            wait_bytes(ref.at[pl.ds(0, SPEC - SPEC // nl - 1)], sem)

        @pl.when(jnp.logical_not(extra))
        def _():
            wait_bytes(ref.at[pl.ds(0, SPEC - SPEC // nl)], sem)

    def first_level0():
        others_rows(xr, xss.at[1])
        mt[...] = jnp.zeros_like(mt)
        cols = []
        for i in range(4):
            for r in range(NPOLE + 1):
                mt[r + 8:r + 9, :] = xr[r, i:i + 1, :]
            cols.append(mt[...].T)
        own, beside = jnp.concatenate(cols[:2], 0), jnp.concatenate(cols[2:], 0)
        near = pltpu.roll(beside, 1, 1) + pltpu.roll(beside, LEV - 1, 1)
        return (own + 0.1 * near) * keept[...]

    def last_rows():
        loads[2].wait()
        here = lax.rem(lon, half)
        base = lon - here
        for slot in range(NPOLE // half):
            r = slot * half + here
            wait_bytes(rs6.at[slot, pl.ds(0, nl - 1)], r6.at[1 + slot])
            waves = split(rs6[slot].reshape(2 * KW, LEV))

            def one(i, carry):
                at_i = lax.rem(here + i, half)
                p = base + at_i
                stage[slot, at_i] = dot3n((inva[0, p], inva[1, p]), waves)
                to_lon(stage.at[slot, at_i], fin.at[r], fsem.at[0], fsem.at[1], p).start()
                return carry
            lax.fori_loop(1, half, one, 0)
            fin[r] = dot3n((inva[0, lon], inva[1, lon]), waves)

    lane_ok = jnp.logical_or(lane >= 8, jnp.logical_not(polar))
    glane = lax.broadcasted_iota(jnp.int32, (GW, LEV), 1) // 21

    for t in range(1, STEPS + 1):
        src, dst = (fa, fb) if t % 2 else (fb, fa)
        sprev, snow = (sa, sb) if t % 2 else (sb, sa)
        sea, sea_next = (st0, st1) if t % 2 else (st1, st0)
        first = jnp.where(polar, 8 + NPOLE, 2 + t)
        count = jnp.where(polar, -(-(22 - t) // 4), -(-(44 - 2 * t) // 4))

        def grid_rows(i, acc):
            adv = []
            for j in range(4):
                f = first + 4 * i + j
                mid = pl.ds(Q0, QN)
                adv.append(0.6 * src[f, mid, :] + 0.1 * (src[f - 1, mid, :] + src[f + 1, mid, :])
                           + east * src[f, pl.ds(Q0 + 1, QN), :] + west * src[f, pl.ds(Q0 - 1, QN), :])
            new, low = levels(jnp.concatenate(adv, 0))
            for j in range(4):
                f = first + 4 * i + j
                dst[f, pl.ds(Q0, QN), :] = new[j * QN:(j + 1) * QN]
                acc = jnp.where(lane == f, low[j * QN:(j + 1) * QN], acc)
            return acc
        a0t[...] = lax.fori_loop(0, count, grid_rows, jnp.zeros((QN, LEV), f32))

        @pl.when(polar)
        def _():
            if t == STEPS:
                last_rows()
            if t > 1:
                message_wait(fx, fxs, t - 1, 1)
                got = split(fx[t - 1].reshape(nl * GW, LEV))
                res = jnp.zeros((2 * KW, LEV), f32)
                for g in range(GROUPS):
                    tab = (ct[0, pl.ds(2 * KW * g, 2 * KW), :], ct[1, pl.ds(2 * KW * g, 2 * KW), :])
                    res = jnp.where(klane // 21 == g, dot3n(tab, got), res)
                hats = dot(jnp.concatenate(split(res), 1), fold_ref[...])
                hat, near = hats[:, :LEV], hats[:, LEV:]
                add = wave_ref[0] * hat + wave_ref[1] * cour[:, 0:1] * swap(hat, krow) + 0.1 * near
                add = add * keept[...]
                at[...] = add
            if t == 1:
                res = dot3n((inv[0], inv[1]), split(first_level0()))
            else:
                message_wait(ex, exs, t - 1, 1)
                level0 = ex[t - 1, :, pl.ds(0, ko), :].reshape(2 * KW, LEV) + vrow0[:, 0:1] * add
                edge = ex[t - 1, :, pl.ds(ko, ko), :].reshape(2 * KW, LEV)
                if t > 2:
                    for i in range(2):
                        vec = vecs[i:i + 1, :]
                        level0 = level0 + vec[:, 0:1] * twice[i]
                        edge = edge + twice[i][:, 7 + NPOLE:8 + NPOLE] * vec
                edge = edge + add[:, 7 + NPOLE:8 + NPOLE] * vrow0 if t < STEPS else add
                res = dot3((inv[0], inv[1]), split(jnp.concatenate([level0, edge], 1)))
            filtered = jnp.logical_and(lane >= 8, lane < 8 + NPOLE)
            a0t[...] = jnp.where(filtered, res[:, :LEV], a0t[...])
            if t == STEPS:
                at[pl.ds(0, QN), :] = res[:, LEV:]
            elif t > 1:
                dst[7 + NPOLE, pl.ds(Q0, QN), :] = res[:, LEV:]

        now = sea[pl.ds(Q0, QN), :]
        flux = coeft[...] * (now - a0t[...])
        fluxt[...] = flux

        if t < STEPS:
            @pl.when(polar)
            def _():
                msg = jnp.zeros((GW, LEV), f32)
                for g in range(GROUPS):
                    turned = pltpu.roll(fluxt[pl.ds(8 + STARTS[g], GW), :], (21 * g - 8) % LEV, 1)
                    msg = jnp.where(glane == g, turned, msg)
                fp[t] = msg
                message(fx, fp, fxs, t)
                if t == 1:
                    others_rows(sa, kss.at[1])
                    evolve(SPEC - 1, sa, sb, 0)
                    message(ex, ep, exs, 0)
                else:
                    own = at[mine, :]
                    for r in range(SPEC - t):
                        snow[r + 1] = snow[r + 1] + own[:, r + 8:r + 9] * vrow0
                evolve(SPEC - 1 - t, snow, sprev, 1 if t == 1 else None)
                if t == 1:
                    message(ex, ep, exs, 1)
                if t < STEPS - 1:
                    evolve(NPOLE, sprev, None, t + 1)
                    message(ex, ep, exs, t + 1)
                if 1 < t:
                    add = at[...]
                    near = pltpu.roll(add, 1, 1) + pltpu.roll(add, LEV - 1, 1)
                    twice[0] = (wave_ref[0] * add + 0.1 * near) * keept[...]
                    twice[1] = wave_ref[1] * swap(add, krow) * keept[...]
                if t == STEPS - 1:
                    def hand_on(dev):
                        for slot in range(NPOLE // half):
                            to_lon(sprev.at[slot * half + lax.rem(dev, half) + 1], rs6.at[slot, lon], r6.at[0], r6.at[1 + slot], dev).start()
                    peers(hand_on)
                    for slot in range(NPOLE // half):
                        rs6[slot, lon] = sprev[slot * half + lax.rem(lon, half) + 1]

        around = (pltpu.roll(now, 1, 1) + pltpu.roll(now, LEV - 1, 1)
                  + sea[pl.ds(Q0 - 1, QN), :] + sea[pl.ds(Q0 + 1, QN), :])
        later = now - 0.3 * flux + 0.2 * (around - 4.0 * now)
        sea_next[pl.ds(Q0, QN), :] = jnp.where(lane_ok, later, 0.0)

        if t == 1:
            @pl.when(polar)
            def _():
                message_wait(ex, exs, 0, 1)
                edge = ex[0, :, pl.ds(ko, ko), :].reshape(2 * KW, LEV)
                dst[7 + NPOLE, pl.ds(Q0, QN), :] = dot3n((inv[0], inv[1]), split(edge))

        def warm(f):
            dst[f, pl.ds(Q0, QN), :] = dst[f, pl.ds(Q0, QN), :] + fluxt[:, f:f + 1] * half0

        def warm_all():
            @pl.when(jnp.logical_not(polar))
            def _():
                for f in range(2 + t, 7 + NPOLE):
                    warm(f)
            for f in range(7 + NPOLE, 46 - t):
                warm(f)
        if t < STEPS:
            warm_all()

    last, sea = fa, st0

    mt[...] = sea[pl.ds(16, LEV), :].T

    def put_row(n, carry):
        seaf[n] = mt[pl.ds(natural(n) + 8, 1), :]
        return carry
    lax.fori_loop(0, ROWS, put_row, 0)
    peers(lambda p: to_lon(seaf.at[pl.ds(rp * p, rp)], seafin.at[lon], fins.at[0], fins.at[1], p).start())

    def own_fin(i, carry):
        seafin[lon, i] = seaf[rp * lon + i]
        return carry
    lax.fori_loop(0, rp, own_fin, 0)

    warm_all()

    def give_grid(m, carry):
        out_ref[natural(m)] = last[m + 8, pl.ds(16, COLS), :]
        return carry
    lax.fori_loop(jnp.where(polar, NPOLE, 0), ROWS, give_grid, 0)

    def row_out(m):
        n = natural(m)
        pltpu.make_async_copy(out_ref.at[n], out_hbm.at[:, n, :], osem).start()

    for m in range(NPOLE, ROWS):
        row_out(m)

    @pl.when(jnp.logical_not(polar))
    def _():
        for m in range(NPOLE):
            row_out(m)

    @pl.when(polar)
    def _():
        wait_bytes(fin.at[pl.ds(0, NPOLE - NPOLE // half)], fsem.at[1])
        for r in range(NPOLE):
            out_ref[natural(r)] = (fin[r] + at[pl.ds(8, COLS), r + 8:r + 9] * vrow0
                                   + fluxt[pl.ds(8, COLS), r + 8:r + 9] * half0)
            row_out(r)

    wait_bytes(seafin.at[pl.ds(0, nl - 1)], fins.at[1])
    for d in range(nl):
        for i in range(rp):
            seaout_ref[i:i + 1, d * COLS:d * COLS + COLS] = seafin[d, i, :, 0:COLS]

    wait_bytes(out_ref, osem)
    wait_bytes(seafin.at[pl.ds(0, nl - 1)], fins.at[0])
    wait_bytes(seab.at[pl.ds(0, ROWS - rp)], seas.at[0])
    lat_sent(halo, asem)
    lat_sent(coefr, csem)
    lat_sent(sear, searow)
    to_east.wait_send()
    to_west.wait_send()

    @pl.when(polar)
    def _():
        for r in range(SPEC):
            @pl.when(lon != owner(r))
            def _():
                wait_bytes(a_ref.at[0], rows.at[0])
        for slot in range(-(-SPEC // nl)):
            @pl.when(slot * nl + turn < SPEC)
            def _():
                wait_bytes(spec.at[slot, pl.ds(0, (nl - 1) * ko)], kss.at[0])
                peers(lambda p: wait_bytes(xs.at[slot], xss.at[0]))
        for t in range(STEPS):
            message_wait(ex, exs, t, 0)
        for t in range(1, STEPS):
            message_wait(fx, fxs, t, 0)
        for slot in range(NPOLE // half):
            peers(lambda p: wait_bytes(sa.at[0], r6.at[0]))
        for slot in range(NPOLE // half):
            wait_bytes(stage.at[slot, pl.ds(0, half - 1)], fsem.at[0])


def local(nl, consts, air, sea, land, courant, vmix, cutoffs):
    rp = ROWS // nl
    ko = 2 * KW // nl
    inv, inva, ct, fold, wave = consts
    half = nl // 2
    last = NPOLE // half
    slots = -(-SPEC // nl)
    vm = pl.BlockSpec(memory_space=pltpu.VMEM)
    hbm = pl.BlockSpec(memory_space=pl.ANY)
    dma = pltpu.SemaphoreType.DMA
    v = pltpu.VMEM
    air_out, sea_out = pl.pallas_call(
        functools.partial(kernel, nl),
        out_shape=(jax.ShapeDtypeStruct((COLS, ROWS, LEV), f32),
                   jax.ShapeDtypeStruct((rp, nl * COLS), f32)),
        in_specs=[hbm, vm, vm, vm, vm, pl.BlockSpec(memory_space=pltpu.SMEM), hbm, hbm, hbm, vm, vm],
        out_specs=(hbm, vm),
        scratch_shapes=[
            v((ROWS, COLS, LEV), f32), v((ROWS, COLS, LEV), f32), v((ROWS, 1, LEV), f32), v((nl, rp, 1, LEV), f32),
            v((FRAMES, WIDE, LEV), f32), v((FRAMES, WIDE, LEV), f32),
            v((SPEC + 2, ko, LEV), f32), v((SPEC + 2, ko, LEV), f32),
            v((slots, nl, COLS, LEV), f32), v((slots, 2 * KW, LEV), f32),
            v((STEPS, nl, GW, LEV), f32), v((STEPS, GW, LEV), f32),
            v((STEPS, nl, 2 * ko, LEV), f32), v((STEPS, 2 * ko, LEV), f32),
            v((last, nl, ko, LEV), f32), v((last, half, COLS, LEV), f32), v((NPOLE, COLS, LEV), f32),
            v((slots, 4, LEV), f32), v((SPEC, 4, LEV), f32),
            v((2, HALO, COLS, LEV), f32), v((2, HALO, 1, LEV), f32), v((2, HALO, 1, LEV), f32),
            v((ROWS, 1, LEV), f32), v((ROWS, 1, LEV), f32), v((nl, rp, 1, LEV), f32),
            v((2, FRAMES, 8, LEV), f32), v((2, FRAMES, 8, LEV), f32),
            v((2, QN, 2 * KW), bf16), v((2, nl, COLS, 2 * KW), bf16), v((2, GROUPS * 2 * KW, nl * GW), bf16),
            v((2, 2 * LEV, 2 * LEV), bf16), v((LEV, LEV), f32),
            v((QN, LEV), f32), v((QN, LEV), f32), v((144, LEV), f32), v((144, LEV), f32),
            v((QN, LEV), f32), v((2 * KW, LEV), f32), v((2 * KW, LEV), f32), v((2, 2 * KW, LEV), f32), v((8, LEV), f32),
            dma((3,)), dma((4,)), dma((4,)), dma((2,)), dma((4,)), dma((4,)), dma((1 + slots,)), dma((2,)),
            dma((STEPS, 2)), dma((STEPS, 2)), dma((1 + last,)), dma((2,)), dma((2,)), dma((2,)), dma, dma,
        ],
        compiler_params=pltpu.CompilerParams(
            collective_id=0, has_side_effects=True, vmem_limit_bytes=56 * 1024 * 1024),
    )(air.transpose(1, 0, 2), sea, land, courant.reshape(1, LEV), vmix, cutoffs, inv, inva, ct, fold, wave)
    return air_out.transpose(1, 0, 2), sea_out


def solution(mesh):
    nl = mesh.shape["lon"]
    consts = tuple(jnp.asarray(x) for x in tables(nl))
    placed = (P("lat", "lon", None), P(("lat", "lon"), None), P("lat", "lon"), P(), P(), P())

    def run(*args):
        return jax.shard_map(
            functools.partial(local, nl),
            mesh=mesh,
            in_specs=((P(),) * 5,) + placed,
            out_specs=(P("lat", "lon", None), P(("lat", "lon"), None)),
            check_vma=False,
        )(consts, *args)

    return run
```
